128 devices in a mesh: heads: 8 (over z, core), width: 4 (over y), sae: 4 (over x).
Axes of the slice: x: 4, y: 4, z: 4, core: 2. Of those that a mesh axis runs over, the one named last changes fastest.
Arguments:
- x_in: bfloat16 [512, 4608], P(None, 'width'), may hold values from -64 to 64
- doc_lengths: int32 [4], replicated, may hold values from 1 to 256, 512 in all
- attn_gain: float32 [4608], P('width'), may hold values from 0.25 to 1.75
- w_query: bfloat16 [4608, 4096], P('width', 'heads'), may hold values from -0.09375 to 0.09375
- w_key: bfloat16 [4608, 2048], P('width', 'heads'), may hold values from -0.09375 to 0.09375
- w_value: bfloat16 [4608, 2048], P('width', 'heads'), may hold values from -0.09375 to 0.09375
- w_out: bfloat16 [4096, 4608], P('heads', 'width'), may hold values from -0.09375 to 0.09375
- post_gain: float32 [4608], replicated, may hold values from 0.25 to 1.75
- enc_weight: bfloat16 [4608, 65536], P(None, ('heads', 'width', 'sae')), may hold values from -0.09375 to 0.09375
- enc_bias: float32 [65536], P(('heads', 'width', 'sae')), may hold values from -1.5 to 0.5
- dec_weight: bfloat16 [65536, 4608], P(('heads', 'width', 'sae')), may hold values from -1 to 1
- dec_bias: float32 [4608], replicated, may hold values from -5 to 5
Outputs:
- grad_enc: bfloat16 [4608, 65536], P(None, ('heads', 'width', 'sae'))
- grad_dec: bfloat16 [65536, 4608], P(('heads', 'width', 'sae'))
- total_loss: float32 [], replicated
The draws below stay inside these ranges and needn't reach their ends.
Inputs may be any that keep to these rules, and one draw needn't show every extreme that they name: `doc_lengths`: lengths of the 4 documents packed in order; they sum to 512.
All inputs are finite; a program needn't handle non-finite values.
Results may differ from the reference program's by a relative error of at most 0.02.
Values may be sent and summed in bfloat16 or wider, within the bound.
A program may use at most 128 MiB of HBM per device.

```python
import math
import jax
import jax.numpy as jnp
import numpy as np
from jax import lax

D = 4608
HEADS = 32
KV_HEADS = 16
HEAD_DIM = 128
TOKENS = 512
DOCS = 4
LATENTS = 65536


def draw_x_in(key, part):
    key_base, key_rows = jax.random.split(key, 2)
    column = jnp.arange(D, dtype=jnp.float32) / D
    base = jnp.clip(jax.random.normal(key_base, (TOKENS, D), jnp.float32), -4.0, 4.0)
    col_scale = 10.0 ** (column - 0.5)
    row_scale = 10.0 ** jax.random.uniform(key_rows, (TOKENS, 1), jnp.float32, -0.5, 0.5)
    return jnp.clip(base * row_scale * col_scale[None, :], -64.0, 64.0).astype(jnp.bfloat16)


def draw_dec_weight(key, part):
    key_base = jax.random.fold_in(key, 0)
    index = jnp.arange(LATENTS, dtype=jnp.float32) / LATENTS
    base = jnp.clip(jax.random.normal(key_base, (LATENTS, D), jnp.float32), -4.0, 4.0)
    row_scale = 10.0 ** index
    values = base * row_scale[:, None] * LATENTS ** (-0.5)
    return jnp.clip(values, -1.0, 1.0).astype(jnp.bfloat16)


def block_levels(key, extent, shards, low, high):
    def one(axis_at, blocks):
        heights = jax.random.uniform(jax.random.fold_in(jax.random.fold_in(key, 6), axis_at), (blocks,), jnp.float32, low / len(shards), high / len(shards))
        return jnp.repeat(jnp.exp(heights), extent[axis_at] // blocks).reshape((-1,) + (1,) * (len(extent) - axis_at - 1))

    level = one(*shards[0])
    for cut in shards[1:]:
        level = level * one(*cut)
    return level


def split_up(count, total, limit, lean):
    portions = [(1 << 20) // math.isqrt(standing ** lean) + 1 for standing in range(2, count + 1)]
    spare, given = total - limit - (count - 1), [1] * (count - 1)
    while spare > 0:
        candidates = [i for i in range(count - 1) if given[i] < limit]
        pool, budget = sum([portions[i] for i in candidates]), spare
        for i in candidates:
            addition = min(limit - given[i], max(1, budget * portions[i] // pool), spare)
            given[i] = given[i] + addition
            spare = spare - addition
    return np.array([limit] + given)


def ragged_sizes(own_key, count, total, most, lean):
    if count == 2:
        one = jax.random.randint(own_key, (), max(1, total - most), min(most, total - 1) + 1)
        return jnp.stack([one, total - one])
    tallies = jnp.asarray(split_up(count, total, most, lean), jnp.int32)
    twos = (count - 1) // 2
    giver, receiver = tallies[1:1 + 2 * twos:2], tallies[2:2 + 2 * twos:2]
    margin = jnp.minimum(giver - 1, most - receiver)
    moved = jax.random.randint(jax.random.fold_in(own_key, 1), (twos,), 0, 1 << 20) % (margin + 1)
    tallies = tallies.at[1:1 + 2 * twos:2].set(giver - moved).at[2:2 + 2 * twos:2].set(receiver + moved)
    return tallies[jax.random.permutation(jax.random.fold_in(own_key, 2), count)]


def bell_draw(own_key, dims, width, most, cuts=(), held_as=jnp.bfloat16):
    result = width * jax.random.normal(own_key, dims, jnp.float32)
    if cuts:
        result = result * block_levels(own_key, dims, cuts, -0.22, 0.18)
    return jnp.clip(result, -most, most).astype(held_as)


def setup_inputs(seed: int = 0) -> dict:
    splits = jax.random.split(jax.random.key(seed), 13)
    x_in = draw_x_in(jax.random.fold_in(splits[12], 71), 0)
    doc_lengths = ragged_sizes(splits[1], DOCS, TOKENS, TOKENS // 2, 2).astype(jnp.int32)
    attn_gain = jnp.clip(1.0 + 0.15 * jax.random.normal(splits[2], (D,), jnp.float32), 0.25, 1.75)
    w_query = bell_draw(splits[3], (D, HEADS * HEAD_DIM), D ** -0.5, 0.09375, ((0, 4), (1, 8)))
    w_key = bell_draw(splits[4], (D, KV_HEADS * HEAD_DIM), D ** -0.5, 0.09375, ((0, 4), (1, 8)))
    w_value = bell_draw(splits[5], (D, KV_HEADS * HEAD_DIM), D ** -0.5, 0.09375, ((0, 4), (1, 8)))
    w_out = bell_draw(splits[6], (HEADS * HEAD_DIM, D), (HEADS * HEAD_DIM) ** -0.5, 0.09375, ((0, 8), (1, 4)))
    post_gain = jnp.clip(1.0 + 0.15 * jax.random.normal(splits[7], (D,), jnp.float32), 0.25, 1.75)
    enc_weight = bell_draw(splits[8], (D, LATENTS), D ** -0.5, 0.09375, ((1, 128),))
    enc_bias = jnp.clip(-1.5 + 2.0 * jax.random.uniform(splits[9], (LATENTS,), jnp.float32) ** block_levels(splits[9], (LATENTS,), ((0, 128),), -0.2, 0.2), -1.5, 0.5)
    dec_weight = draw_dec_weight(jax.random.fold_in(splits[12], 71), 0)
    dec_bias = bell_draw(splits[11], (D,), 1.0, 5.0, (), jnp.float32)
    return {"x_in": x_in, "doc_lengths": doc_lengths, "attn_gain": attn_gain, "w_query": w_query, "w_key": w_key, "w_value": w_value, "w_out": w_out, "post_gain": post_gain, "enc_weight": enc_weight, "enc_bias": enc_bias, "dec_weight": dec_weight, "dec_bias": dec_bias}


norm_eps = 1e-06
soft_cap = 50.0
rope_base = 10000.0
l1_weight = 3.0

def rotary(values, position):
    half_dim = values.shape[-1] // 2
    frequency = rope_base ** (-2.0 * jnp.arange(half_dim, dtype=jnp.float32) / values.shape[-1])
    angles = position.astype(jnp.float32)[:, None] * frequency[None, :]
    cosine_table = jnp.cos(angles)[:, None, :]
    sine_table = jnp.sin(angles)[:, None, :]
    first_half = values[..., :half_dim]
    second_half = values[..., half_dim:]
    return jnp.concatenate([first_half * cosine_table - second_half * sine_table, second_half * cosine_table + first_half * sine_table], axis=-1)

def attend(query4, key_rows, value_rows, allowed, scale):
    scores = jnp.einsum('tkgd,skd->kgts', query4.astype(jnp.float32), key_rows.astype(jnp.float32)) * scale
    capped = soft_cap * jnp.tanh(scores / soft_cap)
    weights = jnp.where(allowed[None, None], jnp.exp(capped), jnp.float32(0.0))
    totals = lax.optimization_barrier(jnp.sum(weights, axis=-1, keepdims=True))
    probs_bf = (weights / totals).astype(jnp.bfloat16)
    return jnp.einsum('kgts,skd->tkgd', probs_bf.astype(jnp.float32), value_rows.astype(jnp.float32)).astype(jnp.bfloat16)

def reference(x_in, doc_lengths, attn_gain, w_query, w_key, w_value, w_out, post_gain, enc_weight, enc_bias, dec_weight, dec_bias):
    tokens = x_in.shape[0]
    boundary = jnp.cumsum(doc_lengths).astype(jnp.int32)
    position = jnp.arange(tokens, dtype=jnp.int32)
    segment = lax.optimization_barrier(jnp.sum((boundary[None, :] <= position[:, None]).astype(jnp.int32), axis=1))
    allowed = (segment[:, None] == segment[None, :]) & (position[None, :] <= position[:, None])
    x_float = x_in.astype(jnp.float32)
    scaled = (x_float * attn_gain).astype(jnp.bfloat16)
    inverse_rms = lax.rsqrt(lax.optimization_barrier(jnp.sum(x_float * x_float, axis=1)) / D + norm_eps)
    query_raw = jnp.dot(scaled, w_query, preferred_element_type=jnp.float32)
    key_raw = jnp.dot(scaled, w_key, preferred_element_type=jnp.float32)
    value_raw = jnp.dot(scaled, w_value, preferred_element_type=jnp.float32)
    query = rotary((query_raw * inverse_rms[:, None]).reshape(tokens, HEADS, HEAD_DIM), position).astype(jnp.bfloat16)
    key_rows = rotary((key_raw * inverse_rms[:, None]).reshape(tokens, KV_HEADS, HEAD_DIM), position).astype(jnp.bfloat16)
    value_rows = (value_raw * inverse_rms[:, None]).reshape(tokens, KV_HEADS, HEAD_DIM).astype(jnp.bfloat16)
    query4 = query.reshape(tokens, KV_HEADS, HEADS // KV_HEADS, HEAD_DIM)
    mixed = attend(query4, key_rows, value_rows, allowed, (D // HEADS) ** (-0.5))
    attn_proj = jnp.dot(mixed.reshape(tokens, HEADS * HEAD_DIM), w_out, preferred_element_type=jnp.float32).astype(jnp.bfloat16)
    proj_float = attn_proj.astype(jnp.float32)
    inverse_post = lax.rsqrt(lax.optimization_barrier(jnp.sum(proj_float * proj_float, axis=1)) / D + norm_eps)
    resid = (x_float + proj_float * inverse_post[:, None] * post_gain).astype(jnp.bfloat16)
    centered = (resid.astype(jnp.float32) - dec_bias).astype(jnp.bfloat16)
    pre_acts = jnp.dot(centered, enc_weight, preferred_element_type=jnp.float32) + enc_bias
    latent_acts = jnp.maximum(pre_acts, 0.0).astype(jnp.bfloat16)
    recon = jnp.dot(latent_acts, dec_weight, preferred_element_type=jnp.float32) + dec_bias
    error = recon - resid.astype(jnp.float32)
    dec_float = dec_weight.astype(jnp.float32)
    row_norms = jnp.sqrt(lax.optimization_barrier(jnp.sum(dec_float * dec_float, axis=1)) + norm_eps)
    act_sums = lax.optimization_barrier(jnp.sum(latent_acts.astype(jnp.float32), axis=0))
    squares_total = jnp.sum(error * error)
    penalty_total = jnp.sum(act_sums * row_norms)
    total_loss = (squares_total + l1_weight * penalty_total) / (tokens * D)
    grad_recon = (2.0 / tokens * error).astype(jnp.bfloat16)
    upstream = jnp.dot(grad_recon, dec_weight.T, preferred_element_type=jnp.float32)
    grad_pre = jnp.where(pre_acts > 0, upstream + l1_weight * row_norms / tokens, jnp.float32(0.0)).astype(jnp.bfloat16)
    grad_enc = jnp.dot(centered.T, grad_pre, preferred_element_type=jnp.float32).astype(jnp.bfloat16)
    grad_dec = (jnp.dot(latent_acts.T, grad_recon, preferred_element_type=jnp.float32) + l1_weight / tokens * act_sums[:, None] * dec_float / row_norms[:, None]).astype(jnp.bfloat16)
    return (grad_enc, grad_dec, total_loss)
```

```python
import functools

import jax
import jax.numpy as jnp
import numpy as np
from jax import lax
from jax.experimental import pallas as pl
from jax.experimental.pallas import tpu as pltpu
from jax.sharding import PartitionSpec as P

D = 4608
HEADS = 32
HEAD_DIM = 128
TOKENS = 512

norm_eps = 1e-06
soft_cap = 50.0
rope_base = 10000.0
l1_weight = 3.0

MESH = pl.DeviceIdType.MESH
BF = jnp.bfloat16
F32 = jnp.float32
HIGHEST = lax.Precision.HIGHEST

ORDERS = (("y", "x", "z"), ("x", "z", "y"), ("z", "y", "x"))


class Nav:
    def __init__(self):
        self.h = lax.axis_index("heads")
        self.y = lax.axis_index("width")
        self.x = lax.axis_index("sae")
        self.z = self.h // 2
        self.c = self.h % 2

    def index(self, axis):
        return {"x": self.x, "y": self.y, "z": self.z}[axis]

    def peer(self, axis, d):
        if axis == "c":
            return {"heads": self.z * 2 + (1 - self.c)}
        if axis == "h":
            return {"heads": (self.h + d) % 8}
        if axis == "z":
            return {"heads": ((self.z + d) % 4) * 2 + self.c}
        if axis == "y":
            return {"width": (self.y + d) % 4}
        return {"sae": (self.x + d) % 4}


def send(src, dst, ssem, rsem, device):
    copy = pltpu.make_async_remote_copy(
        src_ref=src, dst_ref=dst, send_sem=ssem, recv_sem=rsem, device_id=device, device_id_type=MESH
    )
    copy.start()
    return copy


def barrier(nav):
    sem = pltpu.get_barrier_semaphore()
    peers = [("h", d) for d in range(1, 8)] + [(a, d) for a in "xy" for d in (1, 2, 3)]
    for axis, d in peers:
        pl.semaphore_signal(sem, inc=1, device_id=nav.peer(axis, d), device_id_type=MESH)
    pl.semaphore_wait(sem, len(peers))


def gather_sems():
    dma = pltpu.SemaphoreType.DMA
    return [dma((3, 3)), dma((3, 3)), dma((3, 3)), dma((3, 3)), dma((3, 4, 3)), dma((3, 4, 3)), dma((3, 4, 4)), dma((3, 4, 4))]


def all_gather(nav, full, sems):
    s1, r1, s2, r2, s3, r3, sc, rc = sems
    c = nav.c
    sent, first, second, third, core = [], {}, {}, {}, []
    place = [[nav.index(a) for a in order] for order in ORDERS]

    def share(p, k3, k2, slot3, slot2):
        part = full.at[p, c, k3, k2]
        core.append(send(part, part, sc.at[p, slot3, slot2], rc.at[p, slot3, slot2], nav.peer("c", 1)))

    for p, order in enumerate(ORDERS):
        i1, i2, i3 = place[p]
        block = full.at[p, c, i3, i2, i1]
        for d in (1, 2, 3):
            first[p, d] = send(block, block, s1.at[p, d - 1], r1.at[p, d - 1], nav.peer(order[0], d))
    for p, order in enumerate(ORDERS):
        i1, i2, i3 = place[p]
        for d in (1, 2, 3):
            first[p, d].wait_recv()
        part = full.at[p, c, i3, i2]
        for d in (1, 2, 3):
            second[p, d] = send(part, part, s2.at[p, d - 1], r2.at[p, d - 1], nav.peer(order[1], d))
        for d in (1, 2, 3):
            third[p, 0, d] = send(part, part, s3.at[p, 0, d - 1], r3.at[p, 0, d - 1], nav.peer(order[2], d))
        share(p, i3, i2, 0, 0)
    for e in (1, 3, 2):
        for p, order in enumerate(ORDERS):
            i1, i2, i3 = place[p]
            second[p, e].wait_recv()
            k2 = (i2 + 4 - e) % 4
            part = full.at[p, c, i3, k2]
            for d in (1, 2, 3):
                third[p, e, d] = send(part, part, s3.at[p, e, d - 1], r3.at[p, e, d - 1], nav.peer(order[2], d))
            share(p, i3, k2, 0, e)
    for e in (0, 1, 3, 2):
        for d in (1, 3, 2):
            for p, order in enumerate(ORDERS):
                i1, i2, i3 = place[p]
                third[p, e, d].wait_recv()
                share(p, (i3 + 4 - d) % 4, (i2 + 4 - e) % 4, d, e)
    for copy in core:
        copy.wait_recv()
    for group in (first, second, third):
        for copy in group.values():
            copy.wait_send()
    for copy in core:
        copy.wait_send()


def unpack(full, out, sem):
    for p, order in enumerate(ORDERS):
        where = {a: k for k, a in enumerate(order)}
        for c in range(2):
            for y in range(4):
                for z in range(4):
                    idx = [None, None, None]
                    idx[where["y"]] = y
                    idx[where["z"]] = z
                    idx[where["x"]] = slice(None)
                    src = full.at[p, c, idx[2], idx[1], idx[0]]
                    dst = out.at[:, z, c, :, y * 1152 + p * 384 : y * 1152 + (p + 1) * 384]
                    pltpu.make_async_copy(src, dst, sem).start()
    pltpu.make_async_copy(out, out, sem).wait()


def front_kernel(
    doc_ref, gain_ref, post_ref, bias_ref, x_hbm, cos_hbm, sin_hbm, wq_hbm, wk_hbm, wv_hbm, wo_hbm,
    resid_ref, out_hbm,
    xv, cosv, sinv, wq, wk, wv, wo, lsem,
    part32, part16, got1, ss1, got_ss, s1, r1, s1b, r1b,
    kv, s3, r3, mixed, s5, r5, proj, got7, s7, r7, sq8, got8, s8, r8,
    full, osem, *sems,
):
    nav = Nav()
    h, y, x = nav.h, nav.y, nav.x
    rows = pl.ds(pl.multiple_of(x * 128, 128), 128)
    loads = []
    for k, (src, dst) in enumerate(
        [(x_hbm.at[rows], xv), (wq_hbm, wq), (wk_hbm, wk), (wv_hbm, wv), (cos_hbm.at[rows], cosv), (sin_hbm.at[rows], sinv), (wo_hbm, wo)]
    ):
        copy = pltpu.make_async_copy(src, dst, lsem.at[k])
        copy.start()
        loads.append(copy)
    barrier(nav)
    loads[0].wait()
    xf = xv[...].astype(F32)
    ss1[...] = lax.dot_general(
        jnp.ones((8, 1152), F32), xf * xf, (((1,), (1,)), ((), ())), precision=HIGHEST, preferred_element_type=F32
    )
    square = [send(ss1, got_ss.at[d - 1], s1b.at[d - 1], r1b.at[d - 1], nav.peer("y", d)) for d in (1, 2, 3)]
    scaled = (xf * gain_ref[...]).astype(BF)
    loads[1].wait()
    loads[2].wait()
    loads[3].wait()
    for kvh in range(2):
        cols = slice(kvh * 128, kvh * 128 + 128)
        key = jnp.dot(scaled, wk[:, cols], preferred_element_type=F32)
        val = jnp.dot(scaled, wv[:, cols], preferred_element_type=F32)
        for g in range(2):
            w = kvh * 2 + g
            q = jnp.dot(scaled, wq[:, w * 128 : w * 128 + 128], preferred_element_type=F32)
            for k, t in enumerate((q, key, val)):
                part32[w, :, k * 128 : k * 128 + 128] = t
                part16[w, :, k * 128 : k * 128 + 128] = t.astype(BF)
    moved = [send(part16.at[(y + d) % 4], got1.at[d - 1], s1.at[d - 1], r1.at[d - 1], nav.peer("y", d)) for d in (1, 2, 3)]
    for copy in square:
        copy.wait_recv()
    total = ss1[...] + got_ss[0] + got_ss[1] + got_ss[2]
    spread = lax.dot_general(
        total, jnp.full((8, 128), 0.125, F32), (((0,), (0,)), ((), ())), precision=HIGHEST, preferred_element_type=F32
    )
    inverse = lax.rsqrt(spread / D + norm_eps)
    loads[4].wait()
    loads[5].wait()
    for copy in moved:
        copy.wait_recv()
    qkv = []
    for k in range(3):
        cols = slice(k * 128, k * 128 + 128)
        t = part32[y, :, cols] + got1[0, :, cols].astype(F32) + got1[1, :, cols].astype(F32) + got1[2, :, cols].astype(F32)
        t = t * inverse
        if k < 2:
            t = t * cosv[...] + pltpu.roll(t, 64, 1) * sinv[...]
        qkv.append(t.astype(BF))
    kv[x, :, 0:128] = qkv[1]
    kv[x, :, 128:256] = qkv[2]
    spreads = [send(kv.at[x], kv.at[x], s3.at[d - 1], r3.at[d - 1], nav.peer("x", d)) for d in (1, 2, 3)]
    bounds = []
    run = 0
    for j in range(4):
        run = run + doc_ref[j]
        bounds.append(run)
    qpos = x * 128 + lax.broadcasted_iota(jnp.int32, (128, 512), 0)
    kpos = lax.broadcasted_iota(jnp.int32, (128, 512), 1)
    qseg = sum((b <= qpos).astype(jnp.int32) for b in bounds)
    kseg = sum((b <= kpos).astype(jnp.int32) for b in bounds)
    allowed = (qseg == kseg) & (kpos <= qpos)
    for copy in spreads:
        copy.wait_recv()
    keys = kv[:, :, 0:128].reshape(512, 128)
    vals = kv[:, :, 128:256].reshape(512, 128)
    scores = lax.dot_general(qkv[0], keys, (((1,), (1,)), ((), ())), preferred_element_type=F32) * ((D // HEADS) ** -0.5)
    capped = soft_cap * jnp.tanh(scores / soft_cap)
    weights = jnp.where(allowed, jnp.exp(capped), 0.0)
    probs = (weights / jnp.sum(weights, axis=-1, keepdims=True)).astype(BF)
    mixed[y] = jnp.dot(probs, vals, preferred_element_type=F32).astype(BF)
    mixes = [send(mixed.at[y], mixed.at[y], s5.at[d - 1], r5.at[d - 1], nav.peer("y", d)) for d in (1, 2, 3)]
    loads[6].wait()
    for copy in mixes:
        copy.wait_recv()
    whole = jnp.concatenate([mixed[w] for w in range(4)], axis=1)
    for k in range(3):
        cols = slice(k * 384, k * 384 + 384)
        t = jnp.dot(whole, wo[:, cols], preferred_element_type=F32).astype(BF)
        proj[:, :, cols] = t.reshape(8, 16, 384)
    parts = [send(proj.at[(h + d) % 8], got7.at[d - 1], s7.at[d - 1], r7.at[d - 1], nav.peer("h", d)) for d in range(1, 8)]
    for copy in parts:
        copy.wait_recv()
    acc = proj[h].astype(F32)
    for d in range(7):
        acc = acc + got7[d].astype(F32)
    acc = acc.astype(BF).astype(F32)
    sq8[...] = jnp.broadcast_to(jnp.sum(acc * acc, axis=1, keepdims=True), (16, 128))
    norms = [send(sq8, got8.at[d - 1], s8.at[d - 1], r8.at[d - 1], nav.peer("y", d)) for d in (1, 2, 3)]
    for copy in norms:
        copy.wait_recv()
    tot8 = sq8[...] + got8[0] + got8[1] + got8[2]
    inverse_post = lax.rsqrt(tot8 / D + norm_eps)[:, 0:1]
    own_x = xv[pl.ds(pl.multiple_of(h * 16, 16), 16), :].astype(F32)
    resid = (own_x + acc * inverse_post * post_ref[y]).astype(BF)
    resid_ref[...] = resid
    centered = (resid.astype(F32) - bias_ref[y]).astype(BF)
    for p, order in enumerate(ORDERS):
        i1, i2, i3 = [nav.index(a) for a in order]
        full[p, nav.c, i3, i2, i1] = centered[:, p * 384 : p * 384 + 384]
    all_gather(nav, full, sems)
    for group in (square, moved, spreads, mixes, parts, norms):
        for copy in group:
            copy.wait_send()
    unpack(full, out_hbm, osem)


def front(doc, gain, post, bias, x_in, cos, sin, wq, wk, wv, wo):
    dma = pltpu.SemaphoreType.DMA
    vmem = pl.BlockSpec(memory_space=pltpu.VMEM)
    anyspace = pl.BlockSpec(memory_space=pl.ANY)
    return pl.pallas_call(
        front_kernel,
        name="front",
        out_shape=(jax.ShapeDtypeStruct((16, 1152), BF), jax.ShapeDtypeStruct((4, 4, 2, 16, D), BF)),
        in_specs=[pl.BlockSpec(memory_space=pltpu.SMEM)] + [vmem] * 3 + [anyspace] * 7,
        out_specs=(vmem, anyspace),
        scratch_shapes=[
            pltpu.VMEM((128, 1152), BF), pltpu.VMEM((128, 128), F32), pltpu.VMEM((128, 128), F32),
            pltpu.VMEM((1152, 512), BF), pltpu.VMEM((1152, 256), BF), pltpu.VMEM((1152, 256), BF),
            pltpu.VMEM((512, 1152), BF), dma((7,)),
            pltpu.VMEM((4, 128, 384), F32), pltpu.VMEM((4, 128, 384), BF), pltpu.VMEM((3, 128, 384), BF),
            pltpu.VMEM((8, 128), F32), pltpu.VMEM((3, 8, 128), F32), dma((3,)), dma((3,)), dma((3,)), dma((3,)),
            pltpu.VMEM((4, 128, 256), BF), dma((3,)), dma((3,)),
            pltpu.VMEM((4, 128, 128), BF), dma((3,)), dma((3,)),
            pltpu.VMEM((8, 16, 1152), BF), pltpu.VMEM((7, 16, 1152), BF), dma((7,)), dma((7,)),
            pltpu.VMEM((16, 128), F32), pltpu.VMEM((3, 16, 128), F32), dma((3,)), dma((3,)),
            pltpu.VMEM((3, 2, 4, 4, 4, 16, 384), BF), dma(()),
        ] + gather_sems(),
        compiler_params=pltpu.CompilerParams(collective_id=0, has_side_effects=True, vmem_limit_bytes=60 << 20),
    )(doc, gain, post, bias, x_in, cos, sin, wq, wk, wv, wo)


def back_kernel(
    acts_hbm, dec_hbm, resid_ref, bias_ref, pen_ref,
    out_hbm, loss_ref,
    acts, dec, lsem, part, got0, s0, r0, got3, s3, r3, slab, got2, s2, r2, strip, got1, s1, r1,
    mine, gotl, sl, rl, full, osem, *sems,
):
    nav = Nav()
    c = nav.c
    place = [[nav.index(a) for a in order] for order in ORDERS]
    load_a = pltpu.make_async_copy(acts_hbm, acts, lsem.at[0])
    load_a.start()
    load_d = pltpu.make_async_copy(dec_hbm, dec, lsem.at[1])
    load_d.start()
    barrier(nav)
    load_a.wait()
    load_d.wait()
    left = acts[...]
    for p, order in enumerate(ORDERS):
        where = {a: k for k, a in enumerate(order)}

        def chunk(w, carry, p=p, where=where):
            cols = pl.ds(pl.multiple_of(w * 1152 + p * 384, 128), 384)
            t = jnp.dot(left, dec[:, cols], preferred_element_type=F32).astype(BF)
            for xx in range(4):
                for zz in range(4):
                    for cc in range(2):
                        idx = [None, None, None]
                        idx[where["x"]] = xx
                        idx[where["z"]] = zz
                        idx[where["y"]] = w
                        r = xx * 128 + zz * 32 + cc * 16
                        part[p, cc, idx[2], idx[1], idx[0]] = t[r : r + 16]
            return carry

        lax.fori_loop(0, 4, chunk, 0)
    swap = {}
    for p in range(3):
        for d in (1, 2, 3, 0):
            t3 = (place[p][2] + d) % 4
            swap[p, d] = send(part.at[p, 1 - c, t3], got0.at[p, t3], s0.at[p, d], r0.at[p, d], nav.peer("c", 1))
    third = {}
    for d in (2, 1, 3):
        for p, order in enumerate(ORDERS):
            t3 = (place[p][2] + d) % 4
            swap[p, d].wait_recv()
            part[p, c, t3] = (part[p, c, t3].astype(F32) + got0[p, t3].astype(F32)).astype(BF)
            third[p, d] = send(part.at[p, c, t3], got3.at[p, d - 1], s3.at[p, d - 1], r3.at[p, d - 1], nav.peer(order[2], d))
    second, first = {}, {}
    for p, order in enumerate(ORDERS):
        i1, i2, i3 = place[p]
        swap[p, 0].wait_recv()
        for d in (1, 2, 3):
            third[p, d].wait_recv()
        t = part[p, c, i3].astype(F32) + got0[p, i3].astype(F32)
        for d in range(3):
            t = t + got3[p, d].astype(F32)
        slab[p] = t.astype(BF)
        for d in (2, 1, 3):
            second[p, d] = send(slab.at[p, (i2 + d) % 4], got2.at[p, d - 1], s2.at[p, d - 1], r2.at[p, d - 1], nav.peer(order[1], d))
    for p, order in enumerate(ORDERS):
        i1, i2, i3 = place[p]
        for d in (1, 2, 3):
            second[p, d].wait_recv()
        t = slab[p, i2].astype(F32)
        for d in range(3):
            t = t + got2[p, d].astype(F32)
        strip[p] = t.astype(BF)
        for d in (2, 1, 3):
            first[p, d] = send(strip.at[p, (i1 + d) % 4], got1.at[p, d - 1], s1.at[p, d - 1], r1.at[p, d - 1], nav.peer(order[0], d))
    squares = jnp.zeros((16, 384), F32)
    for p, order in enumerate(ORDERS):
        i1, i2, i3 = place[p]
        cols = slice(p * 384, p * 384 + 384)
        for d in (1, 2, 3):
            first[p, d].wait_recv()
        t = strip[p, i1].astype(F32)
        for d in range(3):
            t = t + got1[p, d].astype(F32)
        error = t + bias_ref[nav.y][:, cols] - resid_ref[:, cols].astype(F32)
        squares = squares + error * error
        full[p, c, i3, i2, i1] = (2.0 / TOKENS * error).astype(BF)
    all_gather(nav, full, sems)
    mine[0] = jnp.broadcast_to(jnp.sum(squares, keepdims=True), (8, 128)) + l1_weight * pen_ref[...]
    losses = []
    for k, (axis, n) in enumerate((("h", 8), ("y", 4), ("x", 4))):
        group = [send(mine.at[k], gotl.at[k, d - 1], sl.at[k, d - 1], rl.at[k, d - 1], nav.peer(axis, d)) for d in range(1, n)]
        total = mine[k]
        for copy in group:
            copy.wait_recv()
        for d in range(n - 1):
            total = total + gotl[k, d]
        mine[k + 1] = total
        losses += group
    loss_ref[...] = mine[3] / (TOKENS * D)
    for group in (swap, third, second, first):
        for copy in group.values():
            copy.wait_send()
    for copy in losses:
        copy.wait_send()
    unpack(full, out_hbm, osem)


def back(acts, dec, resid, bias, pen):
    dma = pltpu.SemaphoreType.DMA
    vmem = pl.BlockSpec(memory_space=pltpu.VMEM)
    anyspace = pl.BlockSpec(memory_space=pl.ANY)
    return pl.pallas_call(
        back_kernel,
        name="back",
        out_shape=(jax.ShapeDtypeStruct((4, 4, 2, 16, D), BF), jax.ShapeDtypeStruct((8, 128), F32)),
        in_specs=[anyspace, anyspace, vmem, vmem, vmem],
        out_specs=(anyspace, vmem),
        scratch_shapes=[
            pltpu.VMEM((512, 512), BF), pltpu.VMEM((512, D), BF), dma((2,)),
            pltpu.VMEM((3, 2, 4, 4, 4, 16, 384), BF), pltpu.VMEM((3, 4, 4, 4, 16, 384), BF), dma((3, 4)), dma((3, 4)),
            pltpu.VMEM((3, 3, 4, 4, 16, 384), BF), dma((3, 3)), dma((3, 3)),
            pltpu.VMEM((3, 4, 4, 16, 384), BF), pltpu.VMEM((3, 3, 4, 16, 384), BF), dma((3, 3)), dma((3, 3)),
            pltpu.VMEM((3, 4, 16, 384), BF), pltpu.VMEM((3, 3, 16, 384), BF), dma((3, 3)), dma((3, 3)),
            pltpu.VMEM((4, 8, 128), F32), pltpu.VMEM((3, 7, 8, 128), F32), dma((3, 7)), dma((3, 7)),
            pltpu.VMEM((3, 2, 4, 4, 4, 16, 384), BF), dma(()),
        ] + gather_sems(),
        compiler_params=pltpu.CompilerParams(collective_id=1, has_side_effects=True, vmem_limit_bytes=60 << 20),
    )(acts, dec, resid, bias, pen)


def rope_tables():
    j = np.arange(HEAD_DIM // 2, dtype=np.float32)
    frequency = np.power(np.float32(rope_base), np.float32(-2.0) * j / np.float32(HEAD_DIM)).astype(np.float32)
    angles = (np.arange(TOKENS, dtype=np.float32)[:, None] * frequency[None, :]).astype(np.float32)
    cos, sin = np.cos(angles).astype(np.float32), np.sin(angles).astype(np.float32)
    return np.concatenate([cos, cos], 1), np.concatenate([-sin, sin], 1)


def per_device(
    x_in, doc_lengths, attn_gain, w_query, w_key, w_value, w_out, post_gain, enc_weight, enc_bias, dec_weight, dec_bias
):
    tokens = TOKENS
    cos, sin = rope_tables()
    bias4 = dec_bias.reshape(4, 1, 1152)
    resid, gathered = front(
        doc_lengths, attn_gain.reshape(1, 1152), post_gain.reshape(4, 1, 1152), bias4, x_in,
        jnp.asarray(cos), jnp.asarray(sin), w_query, w_key, w_value, w_out,
    )
    centered = gathered.reshape(tokens, D)
    pre_acts = jnp.dot(centered, enc_weight, preferred_element_type=F32) + enc_bias
    latent_acts = jnp.maximum(pre_acts, 0.0).astype(BF)
    row_norms = jnp.sqrt(jnp.sum(jnp.square(dec_weight.astype(F32)), axis=1) + norm_eps)
    act_sums = jnp.sum(latent_acts.astype(F32), axis=0)
    penalty_part = jnp.sum(act_sums * row_norms)
    grad_full, loss = back(latent_acts, dec_weight, resid, bias4, penalty_part.reshape(1, 1))
    grad_recon = grad_full.reshape(tokens, D)
    upstream = lax.dot_general(grad_recon, dec_weight, (((1,), (1,)), ((), ())), preferred_element_type=F32)
    grad_pre = jnp.where(pre_acts > 0, upstream + l1_weight * row_norms / tokens, 0.0).astype(BF)
    grad_enc = lax.dot_general(centered, grad_pre, (((0,), (0,)), ((), ())), preferred_element_type=F32).astype(BF)
    decoder_term = lax.dot_general(latent_acts, grad_recon, (((0,), (0,)), ((), ())), preferred_element_type=F32)
    grad_dec = (
        decoder_term + l1_weight / tokens * act_sums[:, None] * dec_weight.astype(F32) / row_norms[:, None]
    ).astype(BF)
    return (grad_enc, grad_dec, loss[0, 0])


def solution(mesh):
    placed = (
        P(None, "width"),
        P(),
        P("width"),
        P("width", "heads"),
        P("width", "heads"),
        P("width", "heads"),
        P("heads", "width"),
        P(),
        P(None, ("heads", "width", "sae")),
        P(("heads", "width", "sae")),
        P(("heads", "width", "sae"), None),
        P(),
    )
    return jax.shard_map(
        per_device,
        mesh=mesh,
        in_specs=placed,
        out_specs=(P(None, ("heads", "width", "sae")), P(("heads", "width", "sae"), None), P()),
        check_vma=False,
    )
```

```python
import functools

import jax
import jax.numpy as jnp
import numpy as np
from jax import lax
from jax.experimental import pallas as pl
from jax.experimental.pallas import tpu as pltpu
from jax.sharding import PartitionSpec as P

D = 4608
HEADS = 32
HEAD_DIM = 128
TOKENS = 512

norm_eps = 1e-06
soft_cap = 50.0
rope_base = 10000.0
l1_weight = 3.0

MESH = pl.DeviceIdType.MESH
BF = jnp.bfloat16
F32 = jnp.float32
HIGHEST = lax.Precision.HIGHEST

ORDERS = (("y", "x", "z"), ("x", "z", "y"), ("z", "y", "x"))


class Nav:
    def __init__(self):
        self.h = lax.axis_index("heads")
        self.y = lax.axis_index("width")
        self.x = lax.axis_index("sae")
        self.z = self.h // 2
        self.c = self.h % 2

    def index(self, axis):
        return {"x": self.x, "y": self.y, "z": self.z}[axis]

    def peer(self, axis, d):
        if axis == "c":
            return {"heads": self.z * 2 + (1 - self.c)}
        if axis == "h":
            return {"heads": (self.h + d) % 8}
        if axis == "z":
            return {"heads": ((self.z + d) % 4) * 2 + self.c}
        if axis == "y":
            return {"width": (self.y + d) % 4}
        return {"sae": (self.x + d) % 4}


def send(src, dst, ssem, rsem, device):
    copy = pltpu.make_async_remote_copy(
        src_ref=src, dst_ref=dst, send_sem=ssem, recv_sem=rsem, device_id=device, device_id_type=MESH
    )
    copy.start()
    return copy


def barrier(nav):
    sem = pltpu.get_barrier_semaphore()
    peers = [("h", d) for d in range(1, 8)] + [(a, d) for a in "xy" for d in (1, 2, 3)]
    for axis, d in peers:
        pl.semaphore_signal(sem, inc=1, device_id=nav.peer(axis, d), device_id_type=MESH)
    pl.semaphore_wait(sem, len(peers))


def gather_sems():
    dma = pltpu.SemaphoreType.DMA
    return [dma((3, 3)), dma((3, 3)), dma((3, 3)), dma((3, 3)), dma((3, 4, 3)), dma((3, 4, 3)), dma((3, 4, 4)), dma((3, 4, 4))]


def all_gather(nav, full, sems, filler, unit):
    s1, r1, s2, r2, s3, r3, sc, rc = sems
    c = nav.c
    first, second, third, core = {}, {}, {}, {}
    place = [[nav.index(a) for a in order] for order in ORDERS]

    def share(p, d, e):
        part = full.at[p, c, (place[p][2] + 4 - d) % 4, (place[p][1] + 4 - e) % 4]
        core[p, d, e] = send(part, part, sc.at[p, d, e], rc.at[p, d, e], nav.peer("c", 1))

    def spread(p, e):
        part = full.at[p, c, place[p][2], (place[p][1] + 4 - e) % 4]
        for d in (2, 1, 3):
            third[p, e, d] = send(part, part, s3.at[p, e, d - 1], r3.at[p, e, d - 1], nav.peer(ORDERS[p][2], d))
        share(p, 0, e)

    def collect(d):
        for e in (0, 1, 3, 2):
            for p in range(3):
                third[p, e, d].wait_recv()
                share(p, d, e)

    def units(d):
        for p in range(3):
            for e in range(4):
                core[p, d, e].wait_recv()
            unit(p, (place[p][2] + 4 - d) % 4)

    for p, order in enumerate(ORDERS):
        i1, i2, i3 = place[p]
        block = full.at[p, c, i3, i2, i1]
        for d in (2, 1, 3):
            first[p, d] = send(block, block, s1.at[p, d - 1], r1.at[p, d - 1], nav.peer(order[0], d))
    filler(0)
    for p, order in enumerate(ORDERS):
        i1, i2, i3 = place[p]
        for d in (1, 2, 3):
            first[p, d].wait_recv()
        part = full.at[p, c, i3, i2]
        for d in (2, 1, 3):
            second[p, d] = send(part, part, s2.at[p, d - 1], r2.at[p, d - 1], nav.peer(order[1], d))
        spread(p, 0)
    filler(1)
    for e in (1, 3, 2):
        for p in range(3):
            second[p, e].wait_recv()
            spread(p, e)
    filler(2)
    units(0)
    collect(1)
    collect(3)
    units(1)
    collect(2)
    units(3)
    units(2)
    for group in (first, second, third, core):
        for copy in group.values():
            copy.wait_send()


def columns(w, p):
    start = w * 1152 + p * 384
    if isinstance(start, int):
        return slice(start, start + 384)
    return pl.ds(pl.multiple_of(start, 128), 384)


def slab_rows(p, k3):
    if p == 0:
        return (slice(None), k3)
    if p == 1:
        return ()
    return (slice(None), slice(None), k3)


def slab_pieces(p, k3):
    if p == 1:
        return [((1, slice(None), k3), k3)]
    if p == 0:
        return [((0, slice(None), k3, slice(None), w), w) for w in range(4)]
    return [((2, slice(None), k3, w), w) for w in range(4)]


def unpack(full, out, sem, p, k3):
    for idx, w in slab_pieces(p, k3):
        rows = slab_rows(p, k3)
        rows = rows + (slice(None),) * (4 - len(rows))
        pltpu.make_async_copy(full.at[idx], out.at[rows + (columns(w, p),)], sem).start()


def flat(t):
    return t.reshape(-1, t.shape[-1])


def row_of(ref, y=None):
    n = ref.shape[0]
    if y is None:
        return jnp.concatenate([ref[j : j + 1] for j in range(n)], axis=1)
    q = n // 4
    rows = []
    for j in range(q):
        t = ref[j : j + 1]
        for k in range(1, 4):
            t = jnp.where(y == k, ref[k * q + j : k * q + j + 1], t)
        rows.append(t)
    return jnp.concatenate(rows, axis=1)


def front(nav, doc_ref, gain_ref, post_ref, bias_row, loads, refs):
    (xv, cosv, sinv, wq, wk, wv, wo, part32, part16, got1, ss1, got_ss, s1, r1, s1b, r1b,
     kv, s3, r3, mixed, s5, r5, proj, got7, s7, r7, sq8, got8, s8, r8) = refs
    h, y, x = nav.h, nav.y, nav.x
    loads["x"].wait()
    xf = xv[...].astype(F32)
    ss1[...] = lax.dot_general(
        jnp.ones((8, 1152), F32), xf * xf, (((1,), (1,)), ((), ())), precision=HIGHEST, preferred_element_type=F32
    )
    square = [send(ss1, got_ss.at[d - 1], s1b.at[d - 1], r1b.at[d - 1], nav.peer("y", d)) for d in (1, 2, 3)]
    scaled = (xf * row_of(gain_ref)).astype(BF)
    for name in ("q", "k", "v"):
        loads[name].wait()
    for kvh in range(2):
        cols = slice(kvh * 128, kvh * 128 + 128)
        key = jnp.dot(scaled, wk[:, cols], preferred_element_type=F32)
        val = jnp.dot(scaled, wv[:, cols], preferred_element_type=F32)
        for g in range(2):
            w = kvh * 2 + g
            q = jnp.dot(scaled, wq[:, w * 128 : w * 128 + 128], preferred_element_type=F32)
            for k, t in enumerate((q, key, val)):
                part32[w, :, k * 128 : k * 128 + 128] = t
                part16[w, :, k * 128 : k * 128 + 128] = t.astype(BF)
    moved = [send(part16.at[(y + d) % 4], got1.at[d - 1], s1.at[d - 1], r1.at[d - 1], nav.peer("y", d)) for d in (2, 1, 3)]
    bounds = []
    run = 0
    for j in range(4):
        run = run + doc_ref[j]
        bounds.append(run)
    qpos = x * 128 + lax.broadcasted_iota(jnp.int32, (128, 512), 0)
    kpos = lax.broadcasted_iota(jnp.int32, (128, 512), 1)
    qseg = sum((b <= qpos).astype(jnp.int32) for b in bounds)
    kseg = sum((b <= kpos).astype(jnp.int32) for b in bounds)
    allowed = (qseg == kseg) & (kpos <= qpos)
    for copy in square:
        copy.wait_recv()
    total = ss1[...] + got_ss[0] + got_ss[1] + got_ss[2]
    spread = lax.dot_general(
        total, jnp.full((8, 128), 0.125, F32), (((0,), (0,)), ((), ())), precision=HIGHEST, preferred_element_type=F32
    )
    inverse = lax.rsqrt(spread / D + norm_eps)
    loads["cos"].wait()
    loads["sin"].wait()
    for copy in moved:
        copy.wait_recv()
    qkv = []
    for k in range(3):
        cols = slice(k * 128, k * 128 + 128)
        t = part32[y, :, cols] + got1[0, :, cols].astype(F32) + got1[1, :, cols].astype(F32) + got1[2, :, cols].astype(F32)
        t = t * inverse
        if k < 2:
            t = t * cosv[...] + pltpu.roll(t, 64, 1) * sinv[...]
        qkv.append(t.astype(BF))
    kv[x, :, 0:128] = qkv[1]
    kv[x, :, 128:256] = qkv[2]
    spreads = [send(kv.at[x], kv.at[x], s3.at[d - 1], r3.at[d - 1], nav.peer("x", d)) for d in (2, 1, 3)]
    for copy in spreads:
        copy.wait_recv()
    keys = kv[:, :, 0:128].reshape(512, 128)
    vals = kv[:, :, 128:256].reshape(512, 128)
    scores = lax.dot_general(qkv[0], keys, (((1,), (1,)), ((), ())), preferred_element_type=F32) * ((D // HEADS) ** -0.5)
    capped = soft_cap * jnp.tanh(scores / soft_cap)
    weights = jnp.where(allowed, jnp.exp(capped), 0.0)
    probs = (weights / jnp.sum(weights, axis=-1, keepdims=True)).astype(BF)
    mixed[y] = jnp.dot(probs, vals, preferred_element_type=F32).astype(BF)
    mixes = [send(mixed.at[y], mixed.at[y], s5.at[d - 1], r5.at[d - 1], nav.peer("y", d)) for d in (2, 1, 3)]
    loads["o"].wait()
    for copy in mixes:
        copy.wait_recv()
    whole = jnp.concatenate([mixed[w] for w in range(4)], axis=1)
    for k in range(3):
        cols = slice(k * 384, k * 384 + 384)
        t = jnp.dot(whole, wo[:, cols], preferred_element_type=F32).astype(BF)
        proj[:, :, cols] = t.reshape(8, 16, 384)
    parts = [send(proj.at[(h + d) % 8], got7.at[d - 1], s7.at[d - 1], r7.at[d - 1], nav.peer("h", d)) for d in range(1, 8)]
    for copy in parts:
        copy.wait_recv()
    acc = proj[h].astype(F32)
    for d in range(7):
        acc = acc + got7[d].astype(F32)
    acc = acc.astype(BF).astype(F32)
    sq8[...] = jnp.broadcast_to(jnp.sum(acc * acc, axis=1, keepdims=True), (16, 128))
    norms = [send(sq8, got8.at[d - 1], s8.at[d - 1], r8.at[d - 1], nav.peer("y", d)) for d in (2, 1, 3)]
    for copy in norms:
        copy.wait_recv()
    inverse_post = lax.rsqrt((sq8[...] + got8[0] + got8[1] + got8[2]) / D + norm_eps)[:, 0:1]
    own_x = xv[pl.ds(pl.multiple_of(h * 16, 16), 16), :].astype(F32)
    resid = (own_x + acc * inverse_post * row_of(post_ref, y)).astype(BF)
    centered = (resid.astype(F32) - bias_row).astype(BF)
    sends = square + moved + spreads + mixes + parts + norms
    return resid, centered, sends


def step_kernel(
    doc_ref, gain_ref, post_ref, bias_ref, ebias_ref, x_hbm, cos_hbm, sin_hbm, wq_hbm, wk_hbm, wv_hbm, wo_hbm,
    enc_hbm, dec_hbm,
    cent_hbm, grad_hbm, acts_ref, gpre_ref, coef_ref, loss_ref,
    enc, dec, lsem, osem, resid_ref, full, pre, norms, norm_row,
    part, got0, s0, r0, got3, s3, r3, slab, got2, s2, r2, strip, got1, s1, r1,
    pool_h, pool_y, pool_x, sl, rl, gfull, *rest,
):
    fsems, gsems, frefs = rest[:8], rest[8:16], rest[16:]
    nav = Nav()
    c, h, y, x = nav.c, nav.h, nav.y, nav.x
    place = [[nav.index(a) for a in order] for order in ORDERS]
    rows = pl.ds(pl.multiple_of(x * 128, 128), 128)
    xv, cosv, sinv, wq, wk, wv, wo = frefs[:7]
    loads = {}
    for k, (name, src, dst) in enumerate([
        ("x", x_hbm.at[rows], xv), ("q", wq_hbm, wq), ("k", wk_hbm, wk), ("v", wv_hbm, wv),
        ("cos", cos_hbm.at[rows], cosv), ("sin", sin_hbm.at[rows], sinv), ("o", wo_hbm, wo),
        ("dec", dec_hbm, dec), ("enc", enc_hbm, enc),
    ]):
        loads[name] = pltpu.make_async_copy(src, dst, lsem.at[k])
        loads[name].start()
    barrier(nav)
    bias_row = row_of(bias_ref, y)
    resid, centered, sends = front(nav, doc_ref, gain_ref, post_ref, bias_row, loads, frefs[:-1])
    resid_ref[...] = resid
    for p in range(3):
        i1, i2, i3 = place[p]
        full[p, c, i3, i2, i1] = centered[:, p * 384 : p * 384 + 384]

    def norms_filler(k):
        if k == 0:
            loads["dec"].wait()
            loads["enc"].wait()

            def body(j, carry):
                r = pl.ds(pl.multiple_of(j * 32, 32), 32)
                t = jnp.zeros((32, 128), F32)
                for m in range(36):
                    v = dec[r, m * 128 : m * 128 + 128].astype(F32)
                    t = t + v * v
                norms[r, :] = t
                return carry

            lax.fori_loop(0, 16, body, 0)
            pre[...] = jnp.zeros(pre.shape, F32)
        if k == 1:
            sums = lax.dot_general(
                jnp.ones((8, 128), F32), norms[...], (((1,), (1,)), ((), ())), precision=HIGHEST, preferred_element_type=F32
            )
            norm_row[...] = jnp.sqrt(sums + norm_eps)

    def encode(p, k3):
        dst = slab_rows(p, k3) + (Ellipsis,)
        t = pre[dst]
        shape = t.shape
        t = flat(t)
        for idx, w in slab_pieces(p, k3):
            t = t + jnp.dot(flat(full[idx]), enc[columns(w, p), :], preferred_element_type=F32)
        pre[dst] = t.reshape(shape)
        unpack(full, cent_hbm, osem.at[0], p, k3)

    all_gather(nav, full, fsems, norms_filler, encode)
    act_sum = jnp.zeros((1, 512), F32)
    ebias = row_of(ebias_ref)
    for k in range(2):
        t = flat(pre[k]) + ebias
        pre[k] = t.reshape(4, 4, 16, 512)
        acts = jnp.maximum(t, 0.0).astype(BF)
        acts_ref[k] = acts.reshape(4, 4, 16, 512)
        act_sum = act_sum + jnp.sum(acts.astype(F32), axis=0, keepdims=True)
    penalty = jnp.sum(act_sum * norm_row[0:1], keepdims=True)
    coef_ref[...] = (l1_weight / TOKENS) * act_sum / norm_row[...]

    swap, third, second, first = {}, {}, {}, {}

    def produce(p, d):
        t3 = (place[p][2] + d) % 4
        left = flat(acts_ref[slab_rows(p, t3) + (Ellipsis,)])
        for idx, w in slab_pieces(p, t3):
            t = jnp.dot(left, dec[:, columns(w, p)], preferred_element_type=F32).astype(BF)
            part[idx] = t.reshape((2, 4, 4, 16, 384) if p == 1 else (2, 4, 16, 384))
        swap[p, d] = send(part.at[p, 1 - c, t3], got0.at[p, t3], s0.at[p, d], r0.at[p, d], nav.peer("c", 1))

    def combine(p, d):
        t3 = (place[p][2] + d) % 4
        swap[p, d].wait_recv()
        if d:
            part[p, c, t3] = (part[p, c, t3].astype(F32) + got0[p, t3].astype(F32)).astype(BF)
            third[p, d] = send(part.at[p, c, t3], got3.at[p, d - 1], s3.at[p, d - 1], r3.at[p, d - 1], nav.peer(ORDERS[p][2], d))

    order = [(p, d) for d in (2, 1, 3, 0) for p in (1, 0, 2)]
    for k, (p, d) in enumerate(order):
        produce(p, d)
        if k:
            combine(*order[k - 1])
    combine(*order[-1])
    for p in range(3):
        i1, i2, i3 = place[p]
        for d in (1, 2, 3):
            third[p, d].wait_recv()
        t = part[p, c, i3].astype(F32) + got0[p, i3].astype(F32)
        for d in range(3):
            t = t + got3[p, d].astype(F32)
        slab[p] = t.astype(BF)
        for d in (2, 1, 3):
            second[p, d] = send(slab.at[p, (i2 + d) % 4], got2.at[p, d - 1], s2.at[p, d - 1], r2.at[p, d - 1], nav.peer(ORDERS[p][1], d))
    for p in range(3):
        i1, i2, i3 = place[p]
        for d in (1, 2, 3):
            second[p, d].wait_recv()
        t = slab[p, i2].astype(F32)
        for d in range(3):
            t = t + got2[p, d].astype(F32)
        strip[p] = t.astype(BF)
        for d in (2, 1, 3):
            first[p, d] = send(strip.at[p, (i1 + d) % 4], got1.at[p, d - 1], s1.at[p, d - 1], r1.at[p, d - 1], nav.peer(ORDERS[p][0], d))
    squares = jnp.zeros((16, 384), F32)
    for p in range(3):
        i1, i2, i3 = place[p]
        cols = slice(p * 384, p * 384 + 384)
        for d in (1, 2, 3):
            first[p, d].wait_recv()
        t = strip[p, i1].astype(F32)
        for d in range(3):
            t = t + got1[p, d].astype(F32)
        error = t + bias_row[:, cols] - resid_ref[:, cols].astype(F32)
        squares = squares + error * error
        gfull[p, c, i3, i2, i1] = (2.0 / TOKENS * error).astype(BF)

    pools = [(pool_h, "h", 8, h), (pool_y, "y", 4, y), (pool_x, "x", 4, x)]
    losses = []

    def pool_send(k):
        pool, axis, n, me = pools[k]
        for d in range(1, n):
            losses.append(send(pool.at[me], pool.at[me], sl.at[k, d - 1], rl.at[k, d - 1], nav.peer(axis, d)))

    def pool_sum(k):
        pool, axis, n, me = pools[k]
        for copy in losses[-(n - 1) :]:
            copy.wait_recv()
        total = pool[0]
        for j in range(1, n):
            total = total + pool[j]
        return total

    def loss_filler(k):
        if k == 0:
            pool_h[h] = jnp.broadcast_to(jnp.sum(squares, keepdims=True), (8, 128)) + l1_weight * penalty
            pool_send(0)
        if k == 1:
            pool_y[y] = pool_sum(0)
            pool_send(1)
        if k == 2:
            pool_x[x] = pool_sum(1)
            pool_send(2)

    upstream = frefs[-1]
    upstream[...] = jnp.zeros(upstream.shape, F32)

    def decode(p, k3):
        dst = slab_rows(p, k3) + (Ellipsis,)
        t = upstream[dst]
        shape = t.shape
        t = flat(t)
        for idx, w in slab_pieces(p, k3):
            t = t + lax.dot_general(
                flat(gfull[idx]), dec[:, columns(w, p)], (((1,), (1,)), ((), ())), preferred_element_type=F32
            )
        upstream[dst] = t.reshape(shape)
        unpack(gfull, grad_hbm, osem.at[1], p, k3)

    all_gather(nav, gfull, gsems, loss_filler, decode)
    loss_ref[...] = pool_sum(2) / (TOKENS * D)
    lift = (l1_weight / TOKENS) * norm_row[0:1]
    for k in range(2):
        t = jnp.where(flat(pre[k]) > 0, flat(upstream[k]) + lift, 0.0).astype(BF)
        gpre_ref[k] = t.reshape(4, 4, 16, 512)
    for group in (swap, third, second, first):
        for copy in group.values():
            copy.wait_send()
    for copy in losses + sends:
        copy.wait_send()
    pltpu.make_async_copy(cent_hbm, cent_hbm, osem.at[0]).wait()
    pltpu.make_async_copy(grad_hbm, grad_hbm, osem.at[1]).wait()


def step(*args):
    dma = pltpu.SemaphoreType.DMA
    vmem = pl.BlockSpec(memory_space=pltpu.VMEM)
    anyspace = pl.BlockSpec(memory_space=pl.ANY)
    V = pltpu.VMEM
    front_scratch = [
        V((128, 1152), BF), V((128, 128), F32), V((128, 128), F32),
        V((1152, 512), BF), V((1152, 256), BF), V((1152, 256), BF), V((512, 1152), BF),
        V((4, 128, 384), F32), V((4, 128, 384), BF), V((3, 128, 384), BF),
        V((8, 128), F32), V((3, 8, 128), F32), dma((3,)), dma((3,)), dma((3,)), dma((3,)),
        V((4, 128, 256), BF), dma((3,)), dma((3,)),
        V((4, 128, 128), BF), dma((3,)), dma((3,)),
        V((8, 16, 1152), BF), V((7, 16, 1152), BF), dma((7,)), dma((7,)),
        V((16, 128), F32), V((3, 16, 128), F32), dma((3,)), dma((3,)),
    ]
    return pl.pallas_call(
        step_kernel,
        name="step",
        out_shape=(
            jax.ShapeDtypeStruct((2, 4, 4, 16, D), BF), jax.ShapeDtypeStruct((2, 4, 4, 16, D), BF),
            jax.ShapeDtypeStruct((2, 4, 4, 16, 512), BF), jax.ShapeDtypeStruct((2, 4, 4, 16, 512), BF),
            jax.ShapeDtypeStruct((8, 512), F32), jax.ShapeDtypeStruct((8, 128), F32),
        ),
        in_specs=[pl.BlockSpec(memory_space=pltpu.SMEM)] + [vmem] * 4 + [anyspace] * 9,
        out_specs=(anyspace, anyspace, vmem, vmem, vmem, vmem),
        scratch_shapes=[
            V((D, 512), BF), V((512, D), BF), dma((9,)), dma((2,)), V((16, 1152), BF),
            V((3, 2, 4, 4, 4, 16, 384), BF), V((2, 4, 4, 16, 512), F32), V((512, 128), F32), V((8, 512), F32),
            V((3, 2, 4, 4, 4, 16, 384), BF), V((3, 4, 4, 4, 16, 384), BF), dma((3, 4)), dma((3, 4)),
            V((3, 3, 4, 4, 16, 384), BF), dma((3, 3)), dma((3, 3)),
            V((3, 4, 4, 16, 384), BF), V((3, 3, 4, 16, 384), BF), dma((3, 3)), dma((3, 3)),
            V((3, 4, 16, 384), BF), V((3, 3, 16, 384), BF), dma((3, 3)), dma((3, 3)),
            V((8, 8, 128), F32), V((4, 8, 128), F32), V((4, 8, 128), F32), dma((3, 7)), dma((3, 7)),
            V((3, 2, 4, 4, 4, 16, 384), BF),
        ] + gather_sems() + gather_sems() + front_scratch + [V((2, 4, 4, 16, 512), F32)],
        compiler_params=pltpu.CompilerParams(collective_id=0, has_side_effects=True, vmem_limit_bytes=60 << 20),
    )(*args)


def rope_tables():
    j = np.arange(HEAD_DIM // 2, dtype=np.float32)
    frequency = np.power(np.float32(rope_base), np.float32(-2.0) * j / np.float32(HEAD_DIM)).astype(np.float32)
    angles = (np.arange(TOKENS, dtype=np.float32)[:, None] * frequency[None, :]).astype(np.float32)
    cos, sin = np.cos(angles).astype(np.float32), np.sin(angles).astype(np.float32)
    return np.concatenate([cos, cos], 1), np.concatenate([-sin, sin], 1)


def per_device(
    x_in, doc_lengths, attn_gain, w_query, w_key, w_value, w_out, post_gain, enc_weight, enc_bias, dec_weight, dec_bias
):
    cos, sin = rope_tables()
    centered, grad_recon, acts, grad_pre, coef, loss = step(
        doc_lengths, attn_gain.reshape(9, 128), post_gain.reshape(36, 128), dec_bias.reshape(36, 128),
        enc_bias.reshape(4, 128), x_in, jnp.asarray(cos), jnp.asarray(sin),
        w_query, w_key, w_value, w_out, enc_weight, dec_weight,
    )
    centered, grad_recon = centered.reshape(TOKENS, D), grad_recon.reshape(TOKENS, D)
    acts, grad_pre = acts.reshape(TOKENS, 512), grad_pre.reshape(TOKENS, 512)
    grad_enc = lax.dot_general(centered, grad_pre, (((0,), (0,)), ((), ())), preferred_element_type=F32).astype(BF)
    decoder_term = lax.dot_general(acts, grad_recon, (((0,), (0,)), ((), ())), preferred_element_type=F32)
    grad_dec = (decoder_term + coef[0][:, None] * dec_weight.astype(F32)).astype(BF)
    return (grad_enc, grad_dec, loss[0, 0])


def solution(mesh):
    placed = (
        P(None, "width"),
        P(),
        P("width"),
        P("width", "heads"),
        P("width", "heads"),
        P("width", "heads"),
        P("heads", "width"),
        P(),
        P(None, ("heads", "width", "sae")),
        P(("heads", "width", "sae")),
        P(("heads", "width", "sae"), None),
        P(),
    )
    return jax.shard_map(
        per_device,
        mesh=mesh,
        in_specs=placed,
        out_specs=(P(None, ("heads", "width", "sae")), P(("heads", "width", "sae"), None), P()),
        check_vma=False,
    )
```

```python
import functools

import jax
import jax.numpy as jnp
import numpy as np
from jax import lax
from jax.experimental import pallas as pl
from jax.experimental.pallas import tpu as pltpu
from jax.sharding import PartitionSpec as P

D = 4608
HEADS = 32
HEAD_DIM = 128
TOKENS = 512

norm_eps = 1e-06
soft_cap = 50.0
rope_base = 10000.0
l1_weight = 3.0

MESH = pl.DeviceIdType.MESH
BF = jnp.bfloat16
F32 = jnp.float32
HIGHEST = lax.Precision.HIGHEST

ORDERS = (("y", "x", "z"), ("x", "z", "y"), ("z", "y", "x"))


class Nav:
    def __init__(self):
        self.h = lax.axis_index("heads")
        self.y = lax.axis_index("width")
        self.x = lax.axis_index("sae")
        self.z = self.h // 2
        self.c = self.h % 2

    def index(self, axis):
        return {"x": self.x, "y": self.y, "z": self.z}[axis]

    def peer(self, axis, d):
        if axis == "c":
            return {"heads": self.z * 2 + (1 - self.c)}
        if axis == "h":
            return {"heads": (self.h + d) % 8}
        if axis == "z":
            return {"heads": ((self.z + d) % 4) * 2 + self.c}
        if axis == "y":
            return {"width": (self.y + d) % 4}
        return {"sae": (self.x + d) % 4}


def send(src, dst, ssem, rsem, device):
    copy = pltpu.make_async_remote_copy(
        src_ref=src, dst_ref=dst, send_sem=ssem, recv_sem=rsem, device_id=device, device_id_type=MESH
    )
    copy.start()
    return copy


def drained(ref, ssem, rsem, device):
    pltpu.make_async_remote_copy(
        src_ref=ref, dst_ref=ref, send_sem=ssem, recv_sem=rsem, device_id=device, device_id_type=MESH
    ).wait_send()


def greet(nav):
    sem = pltpu.get_barrier_semaphore()
    peers = [("h", d) for d in range(1, 8)] + [(a, d) for a in "xy" for d in (1, 2, 3)]
    for axis, d in peers:
        pl.semaphore_signal(sem, inc=1, device_id=nav.peer(axis, d), device_id_type=MESH)
    return lambda: pl.semaphore_wait(sem, len(peers))


def gather_sems():
    dma = pltpu.SemaphoreType.DMA
    return [dma((3,)), dma((3, 3)), dma((3,)), dma((3, 3)), dma((3,)), dma((3, 4, 3)), dma((3,)), dma((3, 4, 4))]


def all_gather(nav, full, sems, filler, unit):
    s1, r1, s2, r2, s3, r3, sc, rc = sems
    c = nav.c
    first, second, third, core = {}, {}, {}, {}
    place = [[nav.index(a) for a in order] for order in ORDERS]

    def share(p, d, e):
        part = full.at[p, c, (place[p][2] + 4 - d) % 4, (place[p][1] + 4 - e) % 4]
        core[p, d, e] = send(part, part, sc.at[p], rc.at[p, d, e], nav.peer("c", 1))

    def pass_on(p, e, d, source):
        part = full.at[p, c, (place[p][2] + 4 - source) % 4, (place[p][1] + 4 - e) % 4]
        slot = d if source == 0 else 2
        third[p, e, slot] = send(part, part, s3.at[p], r3.at[p, e, slot - 1], nav.peer(ORDERS[p][2], d))

    def spread(p, e):
        pass_on(p, e, 1, 0)
        pass_on(p, e, 3, 0)
        share(p, 0, e)

    def collect(e):
        for p in range(3):
            for d in (1, 3):
                third[p, e, d].wait_recv()
                if (e % 2 == 0) == (d == 1):
                    pass_on(p, e, d, d)
                share(p, d, e)

    def units(*ds):
        for p in range(3):
            for d in ds:
                for e in range(4):
                    core[p, d, e].wait_recv()
            unit(p, [(place[p][2] + 4 - d) % 4 for d in ds])

    for p, order in enumerate(ORDERS):
        i1, i2, i3 = place[p]
        block = full.at[p, c, i3, i2, i1]
        for d in (2, 1, 3):
            first[p, d] = send(block, block, s1.at[p], r1.at[p, d - 1], nav.peer(order[0], d))
    filler(0)
    for p, order in enumerate(ORDERS):
        i1, i2, i3 = place[p]
        for d in (1, 3, 2):
            first[p, d].wait_recv()
        part = full.at[p, c, i3, i2]
        for d in (2, 1, 3):
            second[p, d] = send(part, part, s2.at[p], r2.at[p, d - 1], nav.peer(order[1], d))
    for p in range(3):
        spread(p, 0)
    filler(1)
    for e in (1, 3, 2):
        for p in range(3):
            second[p, e].wait_recv()
            spread(p, e)
    collect(0)
    filler(2)
    units(0)
    for e in (1, 3, 2):
        collect(e)
    units(1, 3)
    for e in (0, 1, 3, 2):
        for p in range(3):
            third[p, e, 2].wait_recv()
            share(p, 2, e)
    units(2)

    def drain():
        for p in range(3):
            i1, i2, i3 = place[p]
            drained(full.at[p, c, i3, i2, 0:3], s1.at[p], r1.at[p, 0], nav.peer("c", 1))
            drained(full.at[p, c, i3, 0:3], s2.at[p], r1.at[p, 0], nav.peer("c", 1))
            drained(full.at[p, c, 0:3], s3.at[p], r1.at[p, 0], nav.peer("c", 1))
            drained(full.at[p, c], sc.at[p], r1.at[p, 0], nav.peer("c", 1))

    return drain


def columns(w, p):
    start = w * 1152 + p * 384
    if isinstance(start, int):
        return slice(start, start + 384)
    return pl.ds(pl.multiple_of(start, 128), 384)


def slab_rows(p, k3):
    if p == 0:
        return (slice(None), k3)
    if p == 1:
        return ()
    return (slice(None), slice(None), k3)


def slab_product(p, ks, full, weights, total):
    if p == 1:
        left = jnp.concatenate([flat(full[1, :, k]) for k in ks], axis=1)
        total[...] = (flat(total[...]) + weights(ks, left)).reshape(total.shape)
        return
    take = (lambda k, w: flat(full[0, :, k, :, w])) if p == 0 else (lambda k, w: flat(full[2, :, k, w]))
    left = jnp.concatenate([jnp.concatenate([take(k, w) for w in range(4)], axis=1) for k in ks], axis=0)
    t = weights(range(4), left)
    for j, k in enumerate(ks):
        dst = slab_rows(p, k) + (Ellipsis,)
        total[dst] = total[dst] + t[j * 128 : j * 128 + 128].reshape(2, 4, 16, 512)


def slab_pieces(p, k3):
    if p == 1:
        return [((1, slice(None), k3), k3)]
    if p == 0:
        return [((0, slice(None), k3, slice(None), w), w) for w in range(4)]
    return [((2, slice(None), k3, w), w) for w in range(4)]


def unpack(full, out, sem, p, k3):
    for idx, w in slab_pieces(p, k3):
        rows = slab_rows(p, k3)
        rows = rows + (slice(None),) * (4 - len(rows))
        pltpu.make_async_copy(full.at[idx], out.at[rows + (columns(w, p),)], sem).start()


def flat(t):
    return t.reshape(-1, t.shape[-1])


def row_of(ref, y=None):
    n = ref.shape[0]
    if y is None:
        return jnp.concatenate([ref[j : j + 1] for j in range(n)], axis=1)
    q = n // 4
    rows = []
    for j in range(q):
        t = ref[j : j + 1]
        for k in range(1, 4):
            t = jnp.where(y == k, ref[k * q + j : k * q + j + 1], t)
        rows.append(t)
    return jnp.concatenate(rows, axis=1)


def front(nav, doc_ref, gain_ref, post_ref, bias_row, loads, greeted, norm_piece, refs):
    (xv, cosv, sinv, wq, wk, wv, wo, part32, part16, got1, ss1, got_ss, s1, r1, s1b, r1b,
     kv, s3, r3, mixed, s5, r5, proj, got7, s7, r7, sq8, got8, s8, r8) = refs
    h, y, x = nav.h, nav.y, nav.x
    loads["x"].wait()
    xf = xv[...].astype(F32)
    scaled = (xf * row_of(gain_ref)).astype(BF)
    for name in ("q", "k", "v"):
        loads[name].wait()
    loads["dec"].start()
    loads["enc"].start()
    query = jnp.dot(scaled, wq[...], preferred_element_type=F32)
    key = jnp.dot(scaled, wk[...], preferred_element_type=F32)
    val = jnp.dot(scaled, wv[...], preferred_element_type=F32)
    for w in range(4):
        kvh = w // 2 * 128
        for k, t in enumerate((query[:, w * 128 : w * 128 + 128], key[:, kvh : kvh + 128], val[:, kvh : kvh + 128])):
            part32[w, :, k * 128 : k * 128 + 128] = t
            part16[w, :, k * 128 : k * 128 + 128] = t.astype(BF)
    greeted()
    moved = [send(part16.at[(y + d) % 4], got1.at[d - 1], s1.at[d - 1], r1.at[d - 1], nav.peer("y", d)) for d in (2, 1, 3)]
    ss1[...] = lax.dot_general(
        jnp.ones((8, 1152), F32), xf * xf, (((1,), (1,)), ((), ())), precision=HIGHEST, preferred_element_type=F32
    )
    square = [send(ss1, got_ss.at[d - 1], s1b.at[d - 1], r1b.at[d - 1], nav.peer("y", d)) for d in (1, 2, 3)]
    bounds = []
    run = 0
    for j in range(4):
        run = run + doc_ref[j]
        bounds.append(run)
    qpos = x * 128 + lax.broadcasted_iota(jnp.int32, (128, 512), 0)
    kpos = lax.broadcasted_iota(jnp.int32, (128, 512), 1)
    qseg = sum((b <= qpos).astype(jnp.int32) for b in bounds)
    kseg = sum((b <= kpos).astype(jnp.int32) for b in bounds)
    allowed = (qseg == kseg) & (kpos <= qpos)
    for copy in square:
        copy.wait_recv()
    total = ss1[...] + got_ss[0] + got_ss[1] + got_ss[2]
    spread = lax.dot_general(
        total, jnp.full((8, 128), 0.125, F32), (((0,), (0,)), ((), ())), precision=HIGHEST, preferred_element_type=F32
    )
    inverse = lax.rsqrt(spread / D + norm_eps)
    loads["cos"].wait()
    loads["sin"].wait()
    for copy in moved:
        copy.wait_recv()
    qkv = []
    for k in range(3):
        cols = slice(k * 128, k * 128 + 128)
        t = part32[y, :, cols] + got1[0, :, cols].astype(F32) + got1[1, :, cols].astype(F32) + got1[2, :, cols].astype(F32)
        t = t * inverse
        if k < 2:
            t = t * cosv[...] + pltpu.roll(t, 64, 1) * sinv[...]
        qkv.append(t.astype(BF))
    kv[x, :, 0:128] = qkv[1]
    kv[x, :, 128:256] = qkv[2]
    spreads = [send(kv.at[x], kv.at[x], s3.at[d - 1], r3.at[d - 1], nav.peer("x", d)) for d in (2, 1, 3)]
    loads["dec"].wait()
    norm_piece(0)
    for copy in spreads:
        copy.wait_recv()
    keys = kv[:, :, 0:128].reshape(512, 128)
    vals = kv[:, :, 128:256].reshape(512, 128)
    scores = lax.dot_general(qkv[0], keys, (((1,), (1,)), ((), ())), preferred_element_type=F32) * ((D // HEADS) ** -0.5)
    capped = soft_cap * jnp.tanh(scores / soft_cap)
    weights = jnp.where(allowed, jnp.exp(capped), 0.0)
    probs = (weights / jnp.sum(weights, axis=-1, keepdims=True)).astype(BF)
    mixed[y] = jnp.dot(probs, vals, preferred_element_type=F32).astype(BF)
    mixes = [send(mixed.at[y], mixed.at[y], s5.at[d - 1], r5.at[d - 1], nav.peer("y", d)) for d in (2, 1, 3)]
    loads["o"].wait()
    for copy in mixes:
        copy.wait_recv()
    whole = jnp.concatenate([mixed[w] for w in range(4)], axis=1)
    for k in range(3):
        cols = slice(k * 384, k * 384 + 384)
        t = jnp.dot(whole, wo[:, cols], preferred_element_type=F32).astype(BF)
        proj[:, :, cols] = t.reshape(8, 16, 384)
    parts = [send(proj.at[(h + d) % 8], got7.at[d - 1], s7.at[d - 1], r7.at[d - 1], nav.peer("h", d)) for d in range(1, 8)]
    norm_piece(1)
    for copy in parts:
        copy.wait_recv()
    acc = proj[h].astype(F32)
    for d in range(7):
        acc = acc + got7[d].astype(F32)
    acc = acc.astype(BF).astype(F32)
    sq8[...] = jnp.broadcast_to(jnp.sum(acc * acc, axis=1, keepdims=True), (16, 128))
    norms = [send(sq8, got8.at[d - 1], s8.at[d - 1], r8.at[d - 1], nav.peer("y", d)) for d in (2, 1, 3)]
    norm_piece(2)
    for copy in norms:
        copy.wait_recv()
    inverse_post = lax.rsqrt((sq8[...] + got8[0] + got8[1] + got8[2]) / D + norm_eps)[:, 0:1]
    own_x = xv[pl.ds(pl.multiple_of(h * 16, 16), 16), :].astype(F32)
    resid = (own_x + acc * inverse_post * row_of(post_ref, y)).astype(BF)
    centered = (resid.astype(F32) - bias_row).astype(BF)
    sends = square + moved + spreads + mixes + parts + norms
    return resid, centered, sends


def step_kernel(
    doc_ref, gain_ref, post_ref, bias_ref, ebias_ref, x_hbm, cos_hbm, sin_hbm, wq_hbm, wk_hbm, wv_hbm, wo_hbm,
    enc_hbm, dec_hbm,
    cent_hbm, grad_hbm, flipped_ref, gpre_ref, coef_ref, loss_ref,
    acts_ref, enc, dec, lsem, osem, resid_ref, full, pre, norms, norm_row,
    part, got0, s0, r0, relay, got3, s3, r3, slab, got2, s2, r2, strip, got1, s1, r1,
    pool_h, pool_y, pool_x, sl, rl, gfull, *rest,
):
    fsems, gsems, frefs = rest[:8], rest[8:16], rest[16:]
    nav = Nav()
    c, h, y, x = nav.c, nav.h, nav.y, nav.x
    place = [[nav.index(a) for a in order] for order in ORDERS]
    rows = pl.ds(pl.multiple_of(x * 128, 128), 128)
    xv, cosv, sinv, wq, wk, wv, wo = frefs[:7]
    loads = {}
    for k, (name, src, dst) in enumerate([
        ("x", x_hbm.at[rows], xv), ("q", wq_hbm, wq), ("k", wk_hbm, wk), ("v", wv_hbm, wv),
        ("cos", cos_hbm.at[rows], cosv), ("sin", sin_hbm.at[rows], sinv), ("o", wo_hbm, wo),
        ("dec", dec_hbm, dec), ("enc", enc_hbm, enc),
    ]):
        loads[name] = pltpu.make_async_copy(src, dst, lsem.at[k])
        if k < 7:
            loads[name].start()
    greeted = greet(nav)

    def norm_piece(k):
        if k == 2:
            sums = lax.dot_general(
                jnp.ones((8, 128), F32), norms[...], (((1,), (1,)), ((), ())), precision=HIGHEST, preferred_element_type=F32
            )
            norm_row[...] = jnp.sqrt(sums + norm_eps)
            pre[...] = jnp.zeros(pre.shape, F32)
            return

        def body(j, carry):
            r = pl.ds(pl.multiple_of(j * 32, 32), 32)
            t = jnp.zeros((32, 128), F32)
            for m in range(36):
                v = dec[r, m * 128 : m * 128 + 128].astype(F32)
                t = t + v * v
            norms[r, :] = t
            return carry

        lax.fori_loop(k * 8, k * 8 + 8, body, 0)

    bias_row = row_of(bias_ref, y)
    resid, centered, sends = front(nav, doc_ref, gain_ref, post_ref, bias_row, loads, greeted, norm_piece, frefs[:-1])
    resid_ref[...] = resid
    for p in range(3):
        i1, i2, i3 = place[p]
        full[p, c, i3, i2, i1] = centered[:, p * 384 : p * 384 + 384]

    def before_encode(k):
        if k == 2:
            loads["enc"].wait()

    def encode(p, ks):
        def product(ws, left):
            rows = jnp.concatenate([enc[columns(w, p), :] for w in ws], axis=0)
            return jnp.dot(left, rows, preferred_element_type=F32)

        slab_product(p, ks, full, product, pre)
        for k in ks:
            unpack(full, cent_hbm, osem.at[0], p, k)

    drain_full = all_gather(nav, full, fsems, before_encode, encode)
    act_sum = jnp.zeros((1, 512), F32)
    ebias = row_of(ebias_ref)
    for k in range(2):
        t = flat(pre[k]) + ebias
        pre[k] = t.reshape(4, 4, 16, 512)
        acts = jnp.maximum(t, 0.0).astype(BF)
        acts_ref[k] = acts.reshape(4, 4, 16, 512)
        act_sum = act_sum + jnp.sum(acts.astype(F32), axis=0, keepdims=True)
    penalty = jnp.sum(act_sum * norm_row[0:1], keepdims=True)
    coef_ref[...] = (l1_weight / TOKENS) * act_sum / norm_row[...]

    swap, third, second, first = {}, {}, {}, {}

    def exchange(p, d):
        t3 = (place[p][2] + d) % 4
        swap[p, d] = send(part.at[p, 1 - c, t3], got0.at[p, t3], s0.at[p, d], r0.at[p, d], nav.peer("c", 1))

    def produce(p, *ws):
        cols = jnp.concatenate([dec[:, columns(w, p)] for w in ws], axis=1)
        both = jnp.dot(flat(acts_ref[...]), cols, preferred_element_type=F32).astype(BF)
        for j, w in enumerate(ws):
            t = both[:, j * 384 : j * 384 + 384].reshape(2, 4, 4, 16, 384)
            if p == 1:
                part[1, :, w] = t
            elif p == 0:
                part[0, :, :, :, w] = t
            else:
                for z in range(4):
                    part[2, :, :, w, z] = t[:, z]

    def out3(p, slot, src, dst, d):
        third[p, slot] = send(src, dst, s3.at[p, slot], r3.at[p, slot], nav.peer(ORDERS[p][2], d))

    def chip_sum(p, t3, k):
        return part[p, c, t3, k : k + 2].astype(F32) + got0[p, t3, k : k + 2].astype(F32)

    def far(p):
        t3 = (place[p][2] + 2) % 4
        swap[p, 2].wait_recv()
        for k, d in ((0, 1), (2, 3)):
            half = part.at[p, c, t3, k : k + 2]
            half[...] = chip_sum(p, t3, k).astype(BF)
            out3(p, k // 2, half, relay.at[p, k // 2], d)

    def near(p):
        for d, k in ((1, 2), (3, 0)):
            t3 = (place[p][2] + d) % 4
            swap[p, d].wait_recv()
            half = part.at[p, c, t3, k : k + 2]
            half[...] = chip_sum(p, t3, k).astype(BF)
            out3(p, d + 1, half, got3.at[p, d // 2, k : k + 2], d)

    def joined(p):
        for d, k in ((1, 0), (3, 2)):
            t3 = (place[p][2] + d) % 4
            third[p, d // 2].wait_recv()
            half = part.at[p, c, t3, k : k + 2]
            half[...] = (chip_sum(p, t3, k) + relay[p, d // 2].astype(F32)).astype(BF)
            out3(p, d + 2, half, got3.at[p, d // 2, k : k + 2], d)

    produce(1, (y + 2) % 4)
    exchange(1, 2)
    produce(1, (y + 1) % 4, (y + 3) % 4)
    exchange(1, 1)
    exchange(1, 3)
    produce(0, 0, 1)
    far(1)
    produce(0, 2, 3)
    for d in (2, 1, 3, 0):
        exchange(0, d)
    near(1)
    produce(2, 0, 1)
    far(0)
    near(0)
    produce(2, 2, 3)
    for d in (2, 1, 3, 0):
        exchange(2, d)
    produce(1, y)
    exchange(1, 0)
    far(2)
    near(2)
    joined(1)
    joined(0)
    for k in range(2):
        flipped_ref[:, k * 256 : k * 256 + 256] = flat(acts_ref[k]).T
    joined(2)
    for p in range(3):
        swap[p, 0].wait_recv()
    for p in range(3):
        i1, i2, i3 = place[p]
        for slot in (2, 3, 4, 5):
            third[p, slot].wait_recv()
        t = part[p, c, i3].astype(F32) + got0[p, i3].astype(F32)
        t = t + got3[p, 0].astype(F32) + got3[p, 1].astype(F32)
        slab[p] = t.astype(BF)
        for d in (2, 1, 3):
            second[p, d] = send(slab.at[p, (i2 + d) % 4], got2.at[p, d - 1], s2.at[p, d - 1], r2.at[p, d - 1], nav.peer(ORDERS[p][1], d))
    for p in range(3):
        i1, i2, i3 = place[p]
        for d in (1, 2, 3):
            second[p, d].wait_recv()
        t = slab[p, i2].astype(F32)
        for d in range(3):
            t = t + got2[p, d].astype(F32)
        strip[p] = t.astype(BF)
        for d in (2, 1, 3):
            first[p, d] = send(strip.at[p, (i1 + d) % 4], got1.at[p, d - 1], s1.at[p, d - 1], r1.at[p, d - 1], nav.peer(ORDERS[p][0], d))
    squares = jnp.zeros((16, 384), F32)
    for p in range(3):
        i1, i2, i3 = place[p]
        cols = slice(p * 384, p * 384 + 384)
        for d in (1, 2, 3):
            first[p, d].wait_recv()
        t = strip[p, i1].astype(F32)
        for d in range(3):
            t = t + got1[p, d].astype(F32)
        error = t + bias_row[:, cols] - resid_ref[:, cols].astype(F32)
        squares = squares + error * error
        gfull[p, c, i3, i2, i1] = (2.0 / TOKENS * error).astype(BF)

    pools = [(pool_h, "h", 8, h), (pool_y, "y", 4, y), (pool_x, "x", 4, x)]
    losses = []

    def pool_send(k):
        pool, axis, n, me = pools[k]
        for d in range(1, n):
            losses.append(send(pool.at[me], pool.at[me], sl.at[k, d - 1], rl.at[k, d - 1], nav.peer(axis, d)))

    def pool_sum(k):
        pool, axis, n, me = pools[k]
        for copy in losses[-(n - 1) :]:
            copy.wait_recv()
        total = pool[0]
        for j in range(1, n):
            total = total + pool[j]
        return total

    def loss_filler(k):
        if k == 0:
            pool_h[h] = jnp.broadcast_to(jnp.sum(squares, keepdims=True), (8, 128)) + l1_weight * penalty
            pool_send(0)
        if k == 1:
            pool_y[y] = pool_sum(0)
            pool_send(1)
        if k == 2:
            pool_x[x] = pool_sum(1)
            pool_send(2)

    upstream = frefs[-1]
    upstream[...] = jnp.zeros(upstream.shape, F32)

    def decode(p, ks):
        def product(ws, left):
            cols = jnp.concatenate([dec[:, columns(w, p)] for w in ws], axis=1)
            return lax.dot_general(left, cols, (((1,), (1,)), ((), ())), preferred_element_type=F32)

        slab_product(p, ks, gfull, product, upstream)
        for k in ks:
            unpack(gfull, grad_hbm, osem.at[1], p, k)

    drain_gfull = all_gather(nav, gfull, gsems, loss_filler, decode)
    loss_ref[...] = pool_sum(2) / (TOKENS * D)
    lift = (l1_weight / TOKENS) * norm_row[0:1]
    for k in range(2):
        t = jnp.where(flat(pre[k]) > 0, flat(upstream[k]) + lift, 0.0).astype(BF)
        gpre_ref[k] = t.reshape(4, 4, 16, 512)
    drain_full()
    drain_gfull()
    for group in (swap, third, second, first):
        for copy in group.values():
            copy.wait_send()
    for copy in losses + sends:
        copy.wait_send()
    pltpu.make_async_copy(cent_hbm, cent_hbm, osem.at[0]).wait()
    pltpu.make_async_copy(grad_hbm, grad_hbm, osem.at[1]).wait()


def step(*args):
    dma = pltpu.SemaphoreType.DMA
    vmem = pl.BlockSpec(memory_space=pltpu.VMEM)
    anyspace = pl.BlockSpec(memory_space=pl.ANY)
    V = pltpu.VMEM
    front_scratch = [
        V((128, 1152), BF), V((128, 128), F32), V((128, 128), F32),
        V((1152, 512), BF), V((1152, 256), BF), V((1152, 256), BF), V((512, 1152), BF),
        V((4, 128, 384), F32), V((4, 128, 384), BF), V((3, 128, 384), BF),
        V((8, 128), F32), V((3, 8, 128), F32), dma((3,)), dma((3,)), dma((3,)), dma((3,)),
        V((4, 128, 256), BF), dma((3,)), dma((3,)),
        V((4, 128, 128), BF), dma((3,)), dma((3,)),
        V((8, 16, 1152), BF), V((7, 16, 1152), BF), dma((7,)), dma((7,)),
        V((16, 128), F32), V((3, 16, 128), F32), dma((3,)), dma((3,)),
    ]
    return pl.pallas_call(
        step_kernel,
        name="step",
        out_shape=(
            jax.ShapeDtypeStruct((2, 4, 4, 16, D), BF), jax.ShapeDtypeStruct((2, 4, 4, 16, D), BF),
            jax.ShapeDtypeStruct((512, 512), BF), jax.ShapeDtypeStruct((2, 4, 4, 16, 512), BF),
            jax.ShapeDtypeStruct((8, 512), F32), jax.ShapeDtypeStruct((8, 128), F32),
        ),
        in_specs=[pl.BlockSpec(memory_space=pltpu.SMEM)] + [vmem] * 4 + [anyspace] * 9,
        out_specs=(anyspace, anyspace, vmem, vmem, vmem, vmem),
        scratch_shapes=[
            V((2, 4, 4, 16, 512), BF), V((D, 512), BF), V((512, D), BF), dma((9,)), dma((2,)), V((16, 1152), BF),
            V((3, 2, 4, 4, 4, 16, 384), BF), V((2, 4, 4, 16, 512), F32), V((512, 128), F32), V((8, 512), F32),
            V((3, 2, 4, 4, 4, 16, 384), BF), V((3, 4, 4, 4, 16, 384), BF), dma((3, 4)), dma((3, 4)),
            V((3, 2, 2, 4, 16, 384), BF), V((3, 2, 4, 4, 16, 384), BF), dma((3, 6)), dma((3, 6)),
            V((3, 4, 4, 16, 384), BF), V((3, 3, 4, 16, 384), BF), dma((3, 3)), dma((3, 3)),
            V((3, 4, 16, 384), BF), V((3, 3, 16, 384), BF), dma((3, 3)), dma((3, 3)),
            V((8, 8, 128), F32), V((4, 8, 128), F32), V((4, 8, 128), F32), dma((3, 7)), dma((3, 7)),
            V((3, 2, 4, 4, 4, 16, 384), BF),
        ] + gather_sems() + gather_sems() + front_scratch + [V((2, 4, 4, 16, 512), F32)],
        compiler_params=pltpu.CompilerParams(collective_id=0, has_side_effects=True, vmem_limit_bytes=60 << 20),
    )(*args)


def grads_kernel(cent_ref, gpre_ref, grad_ref, flipped_ref, dec_ref, coef_ref, loss_in, genc_ref, gdec_ref, loss_out, lift):
    @pl.when(pl.program_id(0) == 0)
    def _():
        lift[...] = lax.dot_general(
            coef_ref[...], jnp.full((8, 128), 0.125, F32), (((0,), (0,)), ((), ())), precision=HIGHEST, preferred_element_type=F32
        )
        loss_out[0, 0] = loss_in[0, 0]

    t = jnp.dot(flipped_ref[...], grad_ref[...], preferred_element_type=F32)
    for m in range(t.shape[1] // 128):
        cols = slice(m * 128, m * 128 + 128)
        gdec_ref[:, cols] = (t[:, cols] + lift[...] * dec_ref[:, cols].astype(F32)).astype(BF)
    genc_ref[...] = lax.dot_general(
        cent_ref[...], gpre_ref[...], (((0,), (0,)), ((), ())), preferred_element_type=F32
    ).astype(BF)


def grads(centered, grad_pre, grad_recon, acts, dec, coef, loss):
    tall = pl.BlockSpec((512, 768), lambda j: (0, j))
    square = pl.BlockSpec((512, 512), lambda j: (0, 0))
    return pl.pallas_call(
        grads_kernel,
        name="grads",
        grid=(6,),
        out_shape=(
            jax.ShapeDtypeStruct((D, 512), BF), jax.ShapeDtypeStruct((512, D), BF), jax.ShapeDtypeStruct((1, 1), F32)
        ),
        in_specs=[
            tall, square, tall, square, tall, pl.BlockSpec((8, 512), lambda j: (0, 0)), pl.BlockSpec(memory_space=pltpu.SMEM),
        ],
        out_specs=(pl.BlockSpec((768, 512), lambda j: (j, 0)), tall, pl.BlockSpec(memory_space=pltpu.SMEM)),
        scratch_shapes=[pltpu.VMEM((512, 128), F32)],
        compiler_params=pltpu.CompilerParams(dimension_semantics=("arbitrary",), vmem_limit_bytes=63 << 20),
    )(centered, grad_pre, grad_recon, acts, dec, coef, loss)


def rope_tables():
    j = np.arange(HEAD_DIM // 2, dtype=np.float32)
    frequency = np.power(np.float32(rope_base), np.float32(-2.0) * j / np.float32(HEAD_DIM)).astype(np.float32)
    angles = (np.arange(TOKENS, dtype=np.float32)[:, None] * frequency[None, :]).astype(np.float32)
    cos, sin = np.cos(angles).astype(np.float32), np.sin(angles).astype(np.float32)
    return np.concatenate([cos, cos], 1), np.concatenate([-sin, sin], 1)


def per_device(
    x_in, doc_lengths, attn_gain, w_query, w_key, w_value, w_out, post_gain, enc_weight, enc_bias, dec_weight, dec_bias
):
    cos, sin = rope_tables()
    centered, grad_recon, acts, grad_pre, coef, loss = step(
        doc_lengths, attn_gain.reshape(9, 128), post_gain.reshape(36, 128), dec_bias.reshape(36, 128),
        enc_bias.reshape(4, 128), x_in, jnp.asarray(cos), jnp.asarray(sin),
        w_query, w_key, w_value, w_out, enc_weight, dec_weight,
    )
    centered, grad_recon = centered.reshape(TOKENS, D), grad_recon.reshape(TOKENS, D)
    grad_pre = grad_pre.reshape(TOKENS, 512)
    grad_enc, grad_dec, total = grads(centered, grad_pre, grad_recon, acts, dec_weight, coef, loss)
    return (grad_enc, grad_dec, total.reshape(()))


def solution(mesh):
    placed = (
        P(None, "width"),
        P(),
        P("width"),
        P("width", "heads"),
        P("width", "heads"),
        P("width", "heads"),
        P("heads", "width"),
        P(),
        P(None, ("heads", "width", "sae")),
        P(("heads", "width", "sae")),
        P(("heads", "width", "sae"), None),
        P(),
    )
    return jax.shard_map(
        per_device,
        mesh=mesh,
        in_specs=placed,
        out_specs=(P(None, ("heads", "width", "sae")), P(("heads", "width", "sae"), None), P()),
        check_vma=False,
    )
```

```python
import functools

import jax
import jax.numpy as jnp
import numpy as np
from jax import lax
from jax.experimental import pallas as pl
from jax.experimental.pallas import tpu as pltpu
from jax.sharding import PartitionSpec as P

D = 4608
HEADS = 32
HEAD_DIM = 128
TOKENS = 512

norm_eps = 1e-06
soft_cap = 50.0
rope_base = 10000.0
l1_weight = 3.0

MESH = pl.DeviceIdType.MESH
BF = jnp.bfloat16
F32 = jnp.float32
HIGHEST = lax.Precision.HIGHEST

ORDERS = (("y", "x", "z"), ("x", "z", "y"), ("z", "y", "x"))


class Nav:
    def __init__(self):
        self.h = lax.axis_index("heads")
        self.y = lax.axis_index("width")
        self.x = lax.axis_index("sae")
        self.z = self.h // 2
        self.c = self.h % 2

    def index(self, axis):
        return {"x": self.x, "y": self.y, "z": self.z}[axis]

    def peer(self, axis, d):
        if axis == "c":
            return {"heads": self.z * 2 + (1 - self.c)}
        if axis == "h":
            return {"heads": (self.h + d) % 8}
        if axis == "z":
            return {"heads": ((self.z + d) % 4) * 2 + self.c}
        if axis == "y":
            return {"width": (self.y + d) % 4}
        return {"sae": (self.x + d) % 4}


def send(src, dst, ssem, rsem, device):
    copy = pltpu.make_async_remote_copy(
        src_ref=src, dst_ref=dst, send_sem=ssem, recv_sem=rsem, device_id=device, device_id_type=MESH
    )
    copy.start()
    return copy


def drained(ref, ssem, rsem, device):
    pltpu.make_async_remote_copy(
        src_ref=ref, dst_ref=ref, send_sem=ssem, recv_sem=rsem, device_id=device, device_id_type=MESH
    ).wait_send()


def greet(nav):
    sem = pltpu.get_barrier_semaphore()
    peers = [("h", d) for d in range(1, 8)] + [(a, d) for a in "xy" for d in (1, 2, 3)]
    for axis, d in peers:
        pl.semaphore_signal(sem, inc=1, device_id=nav.peer(axis, d), device_id_type=MESH)
    return lambda: pl.semaphore_wait(sem, len(peers))


def gather_sems():
    dma = pltpu.SemaphoreType.DMA
    return [dma((3,)), dma((3, 3)), dma((3,)), dma((3, 3)), dma((3,)), dma((3, 4, 3)), dma((3,)), dma((3, 4, 4))]


def all_gather(nav, full, sems, filler, unit, whole_strips=False):
    s1, r1, s2, r2, s3, r3, sc, rc = sems
    c = nav.c
    first, second, third, core = {}, {}, {}, {}
    place = [[nav.index(a) for a in order] for order in ORDERS]

    def share(p, d, e):
        part = full.at[p, c, (place[p][2] + 4 - d) % 4, (place[p][1] + 4 - e) % 4]
        core[p, d, e] = send(part, part, sc.at[p], rc.at[p, d, e], nav.peer("c", 1))

    def pass_on(p, e, d, source):
        part = full.at[p, c, (place[p][2] + 4 - source) % 4, (place[p][1] + 4 - e) % 4]
        slot = d if source == 0 else 2
        third[p, e, slot] = send(part, part, s3.at[p], r3.at[p, e, slot - 1], nav.peer(ORDERS[p][2], d))

    def spread(p, e):
        pass_on(p, e, 1, 0)
        pass_on(p, e, 3, 0)
        share(p, 0, e)

    def collect(e):
        for p in range(3):
            for d in (1, 3):
                third[p, e, d].wait_recv()
                if (e % 2 == 0) == (d == 1):
                    pass_on(p, e, d, d)
                share(p, d, e)

    def units(p, *ds):
        for d in ds:
            for e in range(4):
                core[p, d, e].wait_recv()
        unit(p, [(place[p][2] + 4 - d) % 4 for d in ds])

    def relayed(*es):
        for e in es:
            for p in range(3):
                third[p, e, 2].wait_recv()
                share(p, 2, e)

    for p, order in enumerate(ORDERS):
        i1, i2, i3 = place[p]
        block = full.at[p, c, i3, i2, i1]
        for d in (2, 1, 3):
            if whole_strips:
                continue
            first[p, d] = send(block, block, s1.at[p], r1.at[p, d - 1], nav.peer(order[0], d))
    filler(0)
    for p, order in enumerate(ORDERS):
        i1, i2, i3 = place[p]
        for d in (1, 3, 2):
            if not whole_strips:
                first[p, d].wait_recv()
        part = full.at[p, c, i3, i2]
        for d in (2, 1, 3):
            second[p, d] = send(part, part, s2.at[p], r2.at[p, d - 1], nav.peer(order[1], d))
    for p in range(3):
        spread(p, 0)
    filler(1)
    for e in (1, 3, 2):
        for p in range(3):
            second[p, e].wait_recv()
            spread(p, e)
    collect(0)
    filler(2)
    for p in range(3):
        units(p, 0)
    for e in (1, 3, 2):
        collect(e)
    units(0, 1, 3)
    relayed(0)
    units(1, 1, 3)
    relayed(1, 3)
    units(2, 1, 3)
    relayed(2)
    for p in range(3):
        units(p, 2)

    def drain():
        for p in range(3):
            i1, i2, i3 = place[p]
            if not whole_strips:
                drained(full.at[p, c, i3, i2, 0:3], s1.at[p], r1.at[p, 0], nav.peer("c", 1))
            drained(full.at[p, c, i3, 0:3], s2.at[p], r1.at[p, 0], nav.peer("c", 1))
            drained(full.at[p, c, 0:3], s3.at[p], r1.at[p, 0], nav.peer("c", 1))
            drained(full.at[p, c], sc.at[p], r1.at[p, 0], nav.peer("c", 1))

    return drain


def columns(w, p):
    start = w * 1152 + p * 384
    if isinstance(start, int):
        return slice(start, start + 384)
    return pl.ds(pl.multiple_of(start, 128), 384)


def slab_rows(p, k3):
    if p == 0:
        return (slice(None), k3)
    if p == 1:
        return ()
    return (slice(None), slice(None), k3)


def slab_product(p, ks, full, weights, total):
    if p == 1:
        left = jnp.concatenate([flat(full[1, :, k]) for k in ks], axis=1)
        total[...] = (flat(total[...]) + weights(ks, left)).reshape(total.shape)
        return
    take = (lambda k, w: flat(full[0, :, k, :, w])) if p == 0 else (lambda k, w: flat(full[2, :, k, w]))
    left = jnp.concatenate([jnp.concatenate([take(k, w) for w in range(4)], axis=1) for k in ks], axis=0)
    t = weights(range(4), left)
    for j, k in enumerate(ks):
        dst = slab_rows(p, k) + (Ellipsis,)
        total[dst] = total[dst] + t[j * 128 : j * 128 + 128].reshape(2, 4, 16, 512)


def slab_pieces(p, k3):
    if p == 1:
        return [((1, slice(None), k3), k3)]
    if p == 0:
        return [((0, slice(None), k3, slice(None), w), w) for w in range(4)]
    return [((2, slice(None), k3, w), w) for w in range(4)]


def unpack(full, out, sem, p, k3):
    for idx, w in slab_pieces(p, k3):
        rows = slab_rows(p, k3)
        rows = rows + (slice(None),) * (4 - len(rows))
        pltpu.make_async_copy(full.at[idx], out.at[rows + (columns(w, p),)], sem).start()


def flat(t):
    return t.reshape(-1, t.shape[-1])


def row_of(ref, y=None):
    n = ref.shape[0]
    if y is None:
        return jnp.concatenate([ref[j : j + 1] for j in range(n)], axis=1)
    q = n // 4
    rows = []
    for j in range(q):
        t = ref[j : j + 1]
        for k in range(1, 4):
            t = jnp.where(y == k, ref[k * q + j : k * q + j + 1], t)
        rows.append(t)
    return jnp.concatenate(rows, axis=1)


def front(nav, doc_ref, gain_ref, post_ref, bias_row, loads, greeted, norm_piece, refs):
    (xv, cosv, sinv, wq, wk, wv, wo, part32, part16, got1, ss1, got_ss, s1, r1, s1b, r1b,
     kv, s3, r3, mixed, s5, r5, proj, got7, s7, r7, sq8, got8, s8, r8) = refs
    h, y, x = nav.h, nav.y, nav.x
    loads["x"].wait()
    xf = xv[...].astype(F32)
    scaled = (xf * row_of(gain_ref)).astype(BF)
    for name in ("q", "k", "v"):
        loads[name].wait()
    loads["dec"].start()
    loads["enc"].start()
    query = jnp.dot(scaled, wq[...], preferred_element_type=F32)
    key = jnp.dot(scaled, wk[...], preferred_element_type=F32)
    val = jnp.dot(scaled, wv[...], preferred_element_type=F32)
    for w in range(4):
        kvh = w // 2 * 128
        for k, t in enumerate((query[:, w * 128 : w * 128 + 128], key[:, kvh : kvh + 128], val[:, kvh : kvh + 128])):
            part32[w, :, k * 128 : k * 128 + 128] = t
            part16[w, :, k * 128 : k * 128 + 128] = t.astype(BF)
    greeted()
    moved = [send(part16.at[(y + d) % 4], got1.at[d - 1], s1.at[d - 1], r1.at[d - 1], nav.peer("y", d)) for d in (2, 1, 3)]
    ss1[...] = lax.dot_general(
        jnp.ones((8, 1152), F32), xf * xf, (((1,), (1,)), ((), ())), precision=HIGHEST, preferred_element_type=F32
    )
    square = [send(ss1, got_ss.at[d - 1], s1b.at[d - 1], r1b.at[d - 1], nav.peer("y", d)) for d in (1, 2, 3)]
    bounds = []
    run = 0
    for j in range(4):
        run = run + doc_ref[j]
        bounds.append(run)
    qpos = x * 128 + lax.broadcasted_iota(jnp.int32, (128, 512), 0)
    kpos = lax.broadcasted_iota(jnp.int32, (128, 512), 1)
    qseg = sum((b <= qpos).astype(jnp.int32) for b in bounds)
    kseg = sum((b <= kpos).astype(jnp.int32) for b in bounds)
    allowed = (qseg == kseg) & (kpos <= qpos)
    for copy in square:
        copy.wait_recv()
    total = ss1[...] + got_ss[0] + got_ss[1] + got_ss[2]
    spread = lax.dot_general(
        total, jnp.full((8, 128), 0.125, F32), (((0,), (0,)), ((), ())), precision=HIGHEST, preferred_element_type=F32
    )
    inverse = lax.rsqrt(spread / D + norm_eps)
    loads["cos"].wait()
    loads["sin"].wait()
    for copy in moved:
        copy.wait_recv()
    qkv = []
    for k in range(3):
        cols = slice(k * 128, k * 128 + 128)
        t = part32[y, :, cols] + got1[0, :, cols].astype(F32) + got1[1, :, cols].astype(F32) + got1[2, :, cols].astype(F32)
        t = t * inverse
        if k < 2:
            t = t * cosv[...] + pltpu.roll(t, 64, 1) * sinv[...]
        qkv.append(t.astype(BF))
    kv[x, :, 0:128] = qkv[1]
    kv[x, :, 128:256] = qkv[2]
    later = []
    for d in (2, 1, 3):
        copy = pltpu.make_async_remote_copy(
            src_ref=kv.at[x], dst_ref=kv.at[x], send_sem=s3.at[d - 1], recv_sem=r3.at[d - 1],
            device_id=nav.peer("x", d), device_id_type=MESH,
        )
        pl.when(x + d < 4)(copy.start)
        later.append((d, copy))
    loads["dec"].wait()
    norm_piece(0)
    for d, copy in later:
        pl.when(x >= d)(copy.wait_recv)
    keys = kv[:, :, 0:128].reshape(512, 128)
    vals = kv[:, :, 128:256].reshape(512, 128)
    scores = lax.dot_general(qkv[0], keys, (((1,), (1,)), ((), ())), preferred_element_type=F32) * ((D // HEADS) ** -0.5)
    capped = soft_cap * jnp.tanh(scores / soft_cap)
    weights = jnp.where(allowed, jnp.exp(capped), 0.0)
    probs = (weights / jnp.sum(weights, axis=-1, keepdims=True)).astype(BF)
    mixed[y] = jnp.dot(probs, vals, preferred_element_type=F32).astype(BF)
    mixes = [send(mixed.at[y], mixed.at[y], s5.at[d - 1], r5.at[d - 1], nav.peer("y", d)) for d in (2, 1, 3)]
    loads["o"].wait()
    for copy in mixes:
        copy.wait_recv()
    whole = jnp.concatenate([mixed[w] for w in range(4)], axis=1)
    for k in range(3):
        cols = slice(k * 384, k * 384 + 384)
        t = jnp.dot(whole, wo[:, cols], preferred_element_type=F32).astype(BF)
        proj[:, :, cols] = t.reshape(8, 16, 384)
    parts = [send(proj.at[(h + d) % 8], got7.at[d - 1], s7.at[d - 1], r7.at[d - 1], nav.peer("h", d)) for d in range(1, 8)]
    norm_piece(1)
    for copy in parts:
        copy.wait_recv()
    acc = proj[h].astype(F32)
    for d in range(7):
        acc = acc + got7[d].astype(F32)
    acc = acc.astype(BF).astype(F32)
    sq8[...] = jnp.broadcast_to(jnp.sum(acc * acc, axis=1, keepdims=True), (16, 128))
    norms = [send(sq8, got8.at[d - 1], s8.at[d - 1], r8.at[d - 1], nav.peer("y", d)) for d in (2, 1, 3)]
    norm_piece(2)
    for copy in norms:
        copy.wait_recv()
    inverse_post = lax.rsqrt((sq8[...] + got8[0] + got8[1] + got8[2]) / D + norm_eps)[:, 0:1]
    own_x = xv[pl.ds(pl.multiple_of(h * 16, 16), 16), :].astype(F32)
    resid = (own_x + acc * inverse_post * row_of(post_ref, y)).astype(BF)
    centered = (resid.astype(F32) - bias_row).astype(BF)
    sends = square + moved + mixes + parts + norms
    return resid, centered, sends, later


def step_kernel(
    doc_ref, gain_ref, post_ref, bias_ref, ebias_ref, x_hbm, cos_hbm, sin_hbm, wq_hbm, wk_hbm, wv_hbm, wo_hbm,
    enc_hbm, dec_hbm,
    cent_hbm, grad_hbm, flipped_ref, gpre_ref, coef_ref, loss_ref,
    acts_ref, enc, dec, lsem, osem, strips, ss, rs, errors, full, pre, norms, norm_row,
    part, got0, s0, r0, relay, got3, s3, r3, slab, got2, s2, r2, got1, s1, r1,
    pool_h, pool_y, pool_x, sl, rl, gfull, *rest,
):
    fsems, gsems, frefs = rest[:8], rest[8:16], rest[16:]
    nav = Nav()
    c, h, y, x = nav.c, nav.h, nav.y, nav.x
    place = [[nav.index(a) for a in order] for order in ORDERS]
    rows = pl.ds(pl.multiple_of(x * 128, 128), 128)
    xv, cosv, sinv, wq, wk, wv, wo = frefs[:7]
    loads = {}
    for k, (name, src, dst) in enumerate([
        ("x", x_hbm.at[rows], xv), ("q", wq_hbm, wq), ("k", wk_hbm, wk), ("v", wv_hbm, wv),
        ("cos", cos_hbm.at[rows], cosv), ("sin", sin_hbm.at[rows], sinv), ("o", wo_hbm, wo),
        ("dec", dec_hbm, dec), ("enc", enc_hbm, enc),
    ]):
        loads[name] = pltpu.make_async_copy(src, dst, lsem.at[k])
        if k < 7:
            loads[name].start()
    kv = frefs[16]
    kv[...] = jnp.zeros(kv.shape, BF)
    greeted = greet(nav)

    def norm_piece(k):
        if k == 2:
            sums = lax.dot_general(
                jnp.ones((8, 128), F32), norms[...], (((1,), (1,)), ((), ())), precision=HIGHEST, preferred_element_type=F32
            )
            norm_row[...] = jnp.sqrt(sums + norm_eps)
            pre[...] = jnp.zeros(pre.shape, F32)
            return

        def body(j, carry):
            r = pl.ds(pl.multiple_of(j * 32, 32), 32)
            t = jnp.zeros((32, 128), F32)
            for m in range(36):
                v = dec[r, m * 128 : m * 128 + 128].astype(F32)
                t = t + v * v
            norms[r, :] = t
            return carry

        lax.fori_loop(k * 8, k * 8 + 8, body, 0)

    bias_row = row_of(bias_ref, y)
    resid, centered, sends, later = front(nav, doc_ref, gain_ref, post_ref, bias_row, loads, greeted, norm_piece, frefs[:-1])
    for p in range(3):
        i1, i2, i3 = place[p]
        full[p, c, i3, i2, i1] = centered[:, p * 384 : p * 384 + 384]
        strips[p, i1] = resid[:, p * 384 : p * 384 + 384]

    def before_encode(k):
        if k == 2:
            loads["enc"].wait()

    def encode(p, ks):
        def product(ws, left):
            rows = jnp.concatenate([enc[columns(w, p), :] for w in ws], axis=0)
            return jnp.dot(left, rows, preferred_element_type=F32)

        slab_product(p, ks, full, product, pre)
        for k in ks:
            unpack(full, cent_hbm, osem.at[0], p, k)

    drain_full = all_gather(nav, full, fsems, before_encode, encode)
    known = {}
    for p, order in enumerate(ORDERS):
        mine = strips.at[p, place[p][0]]
        for d in (2, 1, 3):
            known[p, d] = send(mine, mine, ss.at[p, d - 1], rs.at[p, d - 1], nav.peer(order[0], d))
    act_sum = jnp.zeros((1, 512), F32)
    ebias = row_of(ebias_ref)
    for k in range(2):
        t = flat(pre[k]) + ebias
        pre[k] = t.reshape(4, 4, 16, 512)
        acts = jnp.maximum(t, 0.0).astype(BF)
        acts_ref[k] = acts.reshape(4, 4, 16, 512)
        act_sum = act_sum + jnp.sum(acts.astype(F32), axis=0, keepdims=True)
    penalty = jnp.sum(act_sum * norm_row[0:1], keepdims=True)
    coef_ref[...] = (l1_weight / TOKENS) * act_sum / norm_row[...]

    swap, third, second, first = {}, {}, {}, {}

    def exchange(p, d):
        t3 = (place[p][2] + d) % 4
        swap[p, d] = send(part.at[p, 1 - c, t3], got0.at[p, t3], s0.at[p, d], r0.at[p, d], nav.peer("c", 1))

    def produce(p, *ws):
        cols = jnp.concatenate([dec[:, columns(w, p)] for w in ws], axis=1)
        both = jnp.dot(flat(acts_ref[...]), cols, preferred_element_type=F32).astype(BF)
        for j, w in enumerate(ws):
            t = both[:, j * 384 : j * 384 + 384].reshape(2, 4, 4, 16, 384)
            part[1, :, w] = t

    def out3(p, slot, src, dst, d):
        third[p, slot] = send(src, dst, s3.at[p, slot], r3.at[p, slot], nav.peer(ORDERS[p][2], d))

    def chip_sum(p, t3, k):
        return part[p, c, t3, k : k + 2].astype(F32) + got0[p, t3, k : k + 2].astype(F32)

    def far(p):
        t3 = (place[p][2] + 2) % 4
        swap[p, 2].wait_recv()
        for k, d in ((0, 1), (2, 3)):
            half = part.at[p, c, t3, k : k + 2]
            half[...] = chip_sum(p, t3, k).astype(BF)
            out3(p, k // 2, half, relay.at[p, k // 2], d)

    def near(p):
        for d, k in ((1, 2), (3, 0)):
            t3 = (place[p][2] + d) % 4
            swap[p, d].wait_recv()
            half = part.at[p, c, t3, k : k + 2]
            half[...] = chip_sum(p, t3, k).astype(BF)
            out3(p, d + 1, half, got3.at[p, d // 2, k : k + 2], d)

    def joined(p):
        for d, k in ((1, 0), (3, 2)):
            t3 = (place[p][2] + d) % 4
            third[p, d // 2].wait_recv()
            half = part.at[p, c, t3, k : k + 2]
            half[...] = (chip_sum(p, t3, k) + relay[p, d // 2].astype(F32)).astype(BF)
            out3(p, d + 2, half, got3.at[p, d // 2, k : k + 2], d)

    def produce_rows(p, ds, ws):
        ts = [(place[p][2] + d) % 4 for d in ds]
        left = jnp.concatenate([flat(acts_ref[slab_rows(p, t) + (Ellipsis,)]) for t in ts], axis=0)
        cols = jnp.concatenate([dec[:, columns(w, p)] for w in ws], axis=1)
        both = jnp.dot(left, cols, preferred_element_type=F32).astype(BF)
        for j, t3 in enumerate(ts):
            for i, w in enumerate(ws):
                t = both[j * 128 : j * 128 + 128, i * 384 : i * 384 + 384].reshape(2, 4, 16, 384)
                if p == 0:
                    part[0, :, t3, :, w] = t
                else:
                    part[2, :, t3, w] = t

    produce(1, (y + 2) % 4)
    exchange(1, 2)
    produce_rows(0, (2,), range(4))
    exchange(0, 2)
    produce_rows(2, (2,), range(4))
    exchange(2, 2)
    far(1)
    produce(1, (y + 1) % 4, (y + 3) % 4)
    exchange(1, 1)
    exchange(1, 3)
    far(0)
    far(2)
    produce_rows(0, (1, 3, 0), (0, 1))
    near(1)
    produce_rows(0, (1, 3, 0), (2, 3))
    for d in (1, 3, 0):
        exchange(0, d)
    produce_rows(2, (1, 3, 0), (0, 1))
    near(0)
    produce_rows(2, (1, 3, 0), (2, 3))
    for d in (1, 3, 0):
        exchange(2, d)
    joined(1)
    produce(1, y)
    exchange(1, 0)
    near(2)
    joined(0)
    for k in range(2):
        flipped_ref[:, k * 256 : k * 256 + 256] = flat(acts_ref[k]).T
    joined(2)
    for p in range(3):
        swap[p, 0].wait_recv()
    for p in range(3):
        i1, i2, i3 = place[p]
        for slot in (2, 3, 4, 5):
            third[p, slot].wait_recv()
        t = part[p, c, i3].astype(F32) + got0[p, i3].astype(F32)
        t = t + got3[p, 0].astype(F32) + got3[p, 1].astype(F32)
        slab[p] = t.astype(BF)
        for d in (2, 1, 3):
            second[p, d] = send(slab.at[p, (i2 + d) % 4], got2.at[p, d - 1], s2.at[p, d - 1], r2.at[p, d - 1], nav.peer(ORDERS[p][1], d))
    for p in range(3):
        i1, i2, i3 = place[p]
        for d in (1, 2, 3):
            second[p, d].wait_recv()
        t = slab[p, i2].astype(F32)
        for d in range(3):
            t = t + got2[p, d].astype(F32)
        mine = got1.at[p, i1]
        mine[...] = t.astype(BF)
        for d in (2, 1, 3):
            first[p, d] = send(mine, mine, s1.at[p, d - 1], r1.at[p, d - 1], nav.peer(ORDERS[p][0], d))
    squares = jnp.zeros((16, 384), F32)
    for p in range(3):
        i1, i2, i3 = place[p]
        for d in (1, 2, 3):
            first[p, d].wait_recv()
            known[p, d].wait_recv()
        for j in range(4):
            t = got1[p, 0, j].astype(F32)
            for k in range(1, 4):
                t = t + got1[p, k, j].astype(F32)
            if p == 0:
                bias = jnp.concatenate([bias_ref[j * 9 + k : j * 9 + k + 1] for k in range(3)], axis=1)
            else:
                bias = bias_row[:, p * 384 : p * 384 + 384]
            error = t + bias - strips[p, j].astype(F32)
            errors[j] = error
            gfull[p, c, i3, i2, j] = (2.0 / TOKENS * error).astype(BF)
        own = errors[i1]
        squares = squares + own * own

    pools = [(pool_h, "h", 8, h), (pool_y, "y", 4, y), (pool_x, "x", 4, x)]
    losses = []

    def pool_send(k):
        pool, axis, n, me = pools[k]
        for d in range(1, n):
            losses.append(send(pool.at[me], pool.at[me], sl.at[k, d - 1], rl.at[k, d - 1], nav.peer(axis, d)))

    def pool_sum(k):
        pool, axis, n, me = pools[k]
        for copy in losses[-(n - 1) :]:
            copy.wait_recv()
        total = pool[0]
        for j in range(1, n):
            total = total + pool[j]
        return total

    def loss_filler(k):
        if k == 0:
            pool_h[h] = jnp.broadcast_to(jnp.sum(squares, keepdims=True), (8, 128)) + l1_weight * penalty
            pool_send(0)
        if k == 1:
            pool_y[y] = pool_sum(0)
            pool_send(1)
        if k == 2:
            pool_x[x] = pool_sum(1)
            pool_send(2)

    upstream = frefs[-1]
    upstream[...] = jnp.zeros(upstream.shape, F32)

    def decode(p, ks):
        def product(ws, left):
            cols = jnp.concatenate([dec[:, columns(w, p)] for w in ws], axis=1)
            return lax.dot_general(left, cols, (((1,), (1,)), ((), ())), preferred_element_type=F32)

        slab_product(p, ks, gfull, product, upstream)
        for k in ks:
            unpack(gfull, grad_hbm, osem.at[1], p, k)

    drain_gfull = all_gather(nav, gfull, gsems, loss_filler, decode, whole_strips=True)
    loss_ref[...] = pool_sum(2) / (TOKENS * D)
    lift = (l1_weight / TOKENS) * norm_row[0:1]
    for k in range(2):
        t = jnp.where(flat(pre[k]) > 0, flat(upstream[k]) + lift, 0.0).astype(BF)
        gpre_ref[k] = t.reshape(4, 4, 16, 512)
    drain_full()
    drain_gfull()
    for group in (swap, third, second, first, known):
        for copy in group.values():
            copy.wait_send()
    for copy in losses + sends:
        copy.wait_send()
    for d, copy in later:
        pl.when(x + d < 4)(copy.wait_send)
    pltpu.make_async_copy(cent_hbm, cent_hbm, osem.at[0]).wait()
    pltpu.make_async_copy(grad_hbm, grad_hbm, osem.at[1]).wait()


def step(*args):
    dma = pltpu.SemaphoreType.DMA
    vmem = pl.BlockSpec(memory_space=pltpu.VMEM)
    anyspace = pl.BlockSpec(memory_space=pl.ANY)
    V = pltpu.VMEM
    front_scratch = [
        V((128, 1152), BF), V((128, 128), F32), V((128, 128), F32),
        V((1152, 512), BF), V((1152, 256), BF), V((1152, 256), BF), V((512, 1152), BF),
        V((4, 128, 384), F32), V((4, 128, 384), BF), V((3, 128, 384), BF),
        V((8, 128), F32), V((3, 8, 128), F32), dma((3,)), dma((3,)), dma((3,)), dma((3,)),
        V((4, 128, 256), BF), dma((3,)), dma((3,)),
        V((4, 128, 128), BF), dma((3,)), dma((3,)),
        V((8, 16, 1152), BF), V((7, 16, 1152), BF), dma((7,)), dma((7,)),
        V((16, 128), F32), V((3, 16, 128), F32), dma((3,)), dma((3,)),
    ]
    return pl.pallas_call(
        step_kernel,
        name="step",
        out_shape=(
            jax.ShapeDtypeStruct((2, 4, 4, 16, D), BF), jax.ShapeDtypeStruct((2, 4, 4, 16, D), BF),
            jax.ShapeDtypeStruct((512, 512), BF), jax.ShapeDtypeStruct((2, 4, 4, 16, 512), BF),
            jax.ShapeDtypeStruct((8, 512), F32), jax.ShapeDtypeStruct((8, 128), F32),
        ),
        in_specs=[pl.BlockSpec(memory_space=pltpu.SMEM)] + [vmem] * 4 + [anyspace] * 9,
        out_specs=(anyspace, anyspace, vmem, vmem, vmem, vmem),
        scratch_shapes=[
            V((2, 4, 4, 16, 512), BF), V((D, 512), BF), V((512, D), BF), dma((9,)), dma((2,)), V((3, 4, 16, 384), BF), dma((3, 3)), dma((3, 3)), V((4, 16, 384), F32),
            V((3, 2, 4, 4, 4, 16, 384), BF), V((2, 4, 4, 16, 512), F32), V((512, 128), F32), V((8, 512), F32),
            V((3, 2, 4, 4, 4, 16, 384), BF), V((3, 4, 4, 4, 16, 384), BF), dma((3, 4)), dma((3, 4)),
            V((3, 2, 2, 4, 16, 384), BF), V((3, 2, 4, 4, 16, 384), BF), dma((3, 6)), dma((3, 6)),
            V((3, 4, 4, 16, 384), BF), V((3, 3, 4, 16, 384), BF), dma((3, 3)), dma((3, 3)),
            V((3, 4, 4, 16, 384), BF), dma((3, 3)), dma((3, 3)),
            V((8, 8, 128), F32), V((4, 8, 128), F32), V((4, 8, 128), F32), dma((3, 7)), dma((3, 7)),
            V((3, 2, 4, 4, 4, 16, 384), BF),
        ] + gather_sems() + gather_sems() + front_scratch + [V((2, 4, 4, 16, 512), F32)],
        compiler_params=pltpu.CompilerParams(collective_id=0, has_side_effects=True, vmem_limit_bytes=60 << 20),
    )(*args)


def grads_kernel(cent_ref, gpre_ref, grad_ref, flipped_ref, dec_ref, coef_ref, loss_in, genc_ref, gdec_ref, loss_out, lift):
    @pl.when(pl.program_id(0) == 0)
    def _():
        lift[...] = lax.dot_general(
            coef_ref[...], jnp.full((8, 128), 0.125, F32), (((0,), (0,)), ((), ())), precision=HIGHEST, preferred_element_type=F32
        )
        loss_out[0, 0] = loss_in[0, 0]

    t = jnp.dot(flipped_ref[...], grad_ref[...], preferred_element_type=F32)
    for m in range(t.shape[1] // 128):
        cols = slice(m * 128, m * 128 + 128)
        gdec_ref[:, cols] = (t[:, cols] + lift[...] * dec_ref[:, cols].astype(F32)).astype(BF)
    genc_ref[...] = lax.dot_general(
        cent_ref[...], gpre_ref[...], (((0,), (0,)), ((), ())), preferred_element_type=F32
    ).astype(BF)


def grads(centered, grad_pre, grad_recon, acts, dec, coef, loss):
    tall = pl.BlockSpec((512, 768), lambda j: (0, j))
    square = pl.BlockSpec((512, 512), lambda j: (0, 0))
    return pl.pallas_call(
        grads_kernel,
        name="grads",
        grid=(6,),
        out_shape=(
            jax.ShapeDtypeStruct((D, 512), BF), jax.ShapeDtypeStruct((512, D), BF), jax.ShapeDtypeStruct((1, 1), F32)
        ),
        in_specs=[
            tall, square, tall, square, tall, pl.BlockSpec((8, 512), lambda j: (0, 0)), pl.BlockSpec(memory_space=pltpu.SMEM),
        ],
        out_specs=(pl.BlockSpec((768, 512), lambda j: (j, 0)), tall, pl.BlockSpec(memory_space=pltpu.SMEM)),
        scratch_shapes=[pltpu.VMEM((512, 128), F32)],
        compiler_params=pltpu.CompilerParams(dimension_semantics=("arbitrary",), vmem_limit_bytes=63 << 20),
    )(centered, grad_pre, grad_recon, acts, dec, coef, loss)


def rope_tables():
    j = np.arange(HEAD_DIM // 2, dtype=np.float32)
    frequency = np.power(np.float32(rope_base), np.float32(-2.0) * j / np.float32(HEAD_DIM)).astype(np.float32)
    angles = (np.arange(TOKENS, dtype=np.float32)[:, None] * frequency[None, :]).astype(np.float32)
    cos, sin = np.cos(angles).astype(np.float32), np.sin(angles).astype(np.float32)
    return np.concatenate([cos, cos], 1), np.concatenate([-sin, sin], 1)


def per_device(
    x_in, doc_lengths, attn_gain, w_query, w_key, w_value, w_out, post_gain, enc_weight, enc_bias, dec_weight, dec_bias
):
    cos, sin = rope_tables()
    centered, grad_recon, acts, grad_pre, coef, loss = step(
        doc_lengths, attn_gain.reshape(9, 128), post_gain.reshape(36, 128), dec_bias.reshape(36, 128),
        enc_bias.reshape(4, 128), x_in, jnp.asarray(cos), jnp.asarray(sin),
        w_query, w_key, w_value, w_out, enc_weight, dec_weight,
    )
    centered, grad_recon = centered.reshape(TOKENS, D), grad_recon.reshape(TOKENS, D)
    grad_pre = grad_pre.reshape(TOKENS, 512)
    grad_enc, grad_dec, total = grads(centered, grad_pre, grad_recon, acts, dec_weight, coef, loss)
    return (grad_enc, grad_dec, total.reshape(()))


def solution(mesh):
    placed = (
        P(None, "width"),
        P(),
        P("width"),
        P("width", "heads"),
        P("width", "heads"),
        P("width", "heads"),
        P("heads", "width"),
        P(),
        P(None, ("heads", "width", "sae")),
        P(("heads", "width", "sae")),
        P(("heads", "width", "sae"), None),
        P(),
    )
    return jax.shard_map(
        per_device,
        mesh=mesh,
        in_specs=placed,
        out_specs=(P(None, ("heads", "width", "sae")), P(("heads", "width", "sae"), None), P()),
        check_vma=False,
    )
```

```python
import functools

import jax
import jax.numpy as jnp
import numpy as np
from jax import lax
from jax.experimental import pallas as pl
from jax.experimental.pallas import tpu as pltpu
from jax.sharding import PartitionSpec as P

D = 4608
HEADS = 32
HEAD_DIM = 128
TOKENS = 512

norm_eps = 1e-06
soft_cap = 50.0
rope_base = 10000.0
l1_weight = 3.0

MESH = pl.DeviceIdType.MESH
BF = jnp.bfloat16
F32 = jnp.float32
HIGHEST = lax.Precision.HIGHEST

ORDERS = (("y", "x", "z"), ("x", "z", "y"), ("z", "y", "x"))


class Nav:
    def __init__(self):
        self.h = lax.axis_index("heads")
        self.y = lax.axis_index("width")
        self.x = lax.axis_index("sae")
        self.z = self.h // 2
        self.c = self.h % 2

    def index(self, axis):
        return {"x": self.x, "y": self.y, "z": self.z}[axis]

    def peer(self, axis, d):
        if axis == "c":
            return {"heads": self.z * 2 + (1 - self.c)}
        if axis == "h":
            return {"heads": (self.h + d) % 8}
        if axis == "z":
            return {"heads": ((self.z + d) % 4) * 2 + self.c}
        if axis == "y":
            return {"width": (self.y + d) % 4}
        return {"sae": (self.x + d) % 4}


def send(src, dst, ssem, rsem, device):
    copy = pltpu.make_async_remote_copy(
        src_ref=src, dst_ref=dst, send_sem=ssem, recv_sem=rsem, device_id=device, device_id_type=MESH
    )
    copy.start()
    return copy


def drained(ref, ssem, rsem, device):
    pltpu.make_async_remote_copy(
        src_ref=ref, dst_ref=ref, send_sem=ssem, recv_sem=rsem, device_id=device, device_id_type=MESH
    ).wait_send()


def greet(nav):
    sem = pltpu.get_barrier_semaphore()
    peers = [("h", d) for d in range(1, 8)] + [(a, d) for a in "xy" for d in (1, 2, 3)]
    for axis, d in peers:
        pl.semaphore_signal(sem, inc=1, device_id=nav.peer(axis, d), device_id_type=MESH)
    return lambda: pl.semaphore_wait(sem, len(peers))


def gather_sems():
    dma = pltpu.SemaphoreType.DMA
    return [dma((3,)), dma((3, 3)), dma((3,)), dma((3, 3)), dma((3,)), dma((3, 4, 3)), dma((3,)), dma((3, 4, 4))]


def all_gather(nav, full, sems, filler, unit, whole_strips=False):
    s1, r1, s2, r2, s3, r3, sc, rc = sems
    c = nav.c
    first, second, third, core = {}, {}, {}, {}
    place = [[nav.index(a) for a in order] for order in ORDERS]

    def share(p, d, e):
        part = full.at[p, c, (place[p][2] + 4 - d) % 4, (place[p][1] + 4 - e) % 4]
        core[p, d, e] = send(part, part, sc.at[p], rc.at[p, d, e], nav.peer("c", 1))

    def pass_on(p, e, d, source):
        part = full.at[p, c, (place[p][2] + 4 - source) % 4, (place[p][1] + 4 - e) % 4]
        slot = d if source == 0 else 2
        third[p, e, slot] = send(part, part, s3.at[p], r3.at[p, e, slot - 1], nav.peer(ORDERS[p][2], d))

    def spread(p, e):
        pass_on(p, e, 1, 0)
        pass_on(p, e, 3, 0)
        share(p, 0, e)

    def collect(e):
        for p in range(3):
            for d in (1, 3):
                third[p, e, d].wait_recv()
                if (e % 2 == 0) == (d == 1):
                    pass_on(p, e, d, d)
                share(p, d, e)

    def units(p, *ds):
        for d in ds:
            for e in range(4):
                core[p, d, e].wait_recv()
        unit(p, [(place[p][2] + 4 - d) % 4 for d in ds])

    def relayed(*es):
        for e in es:
            for p in range(3):
                third[p, e, 2].wait_recv()
                share(p, 2, e)

    for p, order in enumerate(ORDERS):
        i1, i2, i3 = place[p]
        block = full.at[p, c, i3, i2, i1]
        for d in (2, 1, 3):
            if whole_strips:
                continue
            first[p, d] = send(block, block, s1.at[p], r1.at[p, d - 1], nav.peer(order[0], d))
    filler(0)
    for p, order in enumerate(ORDERS):
        i1, i2, i3 = place[p]
        for d in (1, 3, 2):
            if not whole_strips:
                first[p, d].wait_recv()
        part = full.at[p, c, i3, i2]
        for d in (2, 1, 3):
            second[p, d] = send(part, part, s2.at[p], r2.at[p, d - 1], nav.peer(order[1], d))
    for p in range(3):
        spread(p, 0)
    filler(1)
    for e in (1, 3, 2):
        for p in range(3):
            second[p, e].wait_recv()
            spread(p, e)
    collect(0)
    filler(2)
    for p in range(3):
        units(p, 0)
    for e in (1, 3, 2):
        collect(e)
    units(0, 1, 3)
    relayed(0)
    units(1, 1, 3)
    relayed(1, 3)
    units(2, 1, 3)
    relayed(2)
    for p in range(3):
        units(p, 2)

    def drain():
        for p in range(3):
            i1, i2, i3 = place[p]
            if not whole_strips:
                drained(full.at[p, c, i3, i2, 0:3], s1.at[p], r1.at[p, 0], nav.peer("c", 1))
            drained(full.at[p, c, i3, 0:3], s2.at[p], r1.at[p, 0], nav.peer("c", 1))
            drained(full.at[p, c, 0:3], s3.at[p], r1.at[p, 0], nav.peer("c", 1))
            drained(full.at[p, c], sc.at[p], r1.at[p, 0], nav.peer("c", 1))

    return drain


def columns(w, p):
    start = w * 1152 + p * 384
    if isinstance(start, int):
        return slice(start, start + 384)
    return pl.ds(pl.multiple_of(start, 128), 384)


def slab_rows(p, k3):
    if p == 0:
        return (slice(None), k3)
    if p == 1:
        return ()
    return (slice(None), slice(None), k3)


def slab_product(p, ks, full, weights, total):
    if p == 1:
        left = jnp.concatenate([flat(full[1, :, k]) for k in ks], axis=1)
        total[...] = (flat(total[...]) + weights(ks, left)).reshape(total.shape)
        return
    take = (lambda k, w: flat(full[0, :, k, :, w])) if p == 0 else (lambda k, w: flat(full[2, :, k, w]))
    left = jnp.concatenate([jnp.concatenate([take(k, w) for w in range(4)], axis=1) for k in ks], axis=0)
    t = weights(range(4), left)
    for j, k in enumerate(ks):
        dst = slab_rows(p, k) + (Ellipsis,)
        total[dst] = total[dst] + t[j * 128 : j * 128 + 128].reshape(2, 4, 16, 512)


def slab_pieces(p, k3):
    if p == 1:
        return [((1, slice(None), k3), k3)]
    if p == 0:
        return [((0, slice(None), k3, slice(None), w), w) for w in range(4)]
    return [((2, slice(None), k3, w), w) for w in range(4)]


def unpack(full, out, sem, p, k3):
    for idx, w in slab_pieces(p, k3):
        rows = slab_rows(p, k3)
        rows = rows + (slice(None),) * (4 - len(rows))
        pltpu.make_async_copy(full.at[idx], out.at[rows + (columns(w, p),)], sem).start()


def flat(t):
    return t.reshape(-1, t.shape[-1])


def row_of(ref, y=None):
    n = ref.shape[0]
    if y is None:
        return jnp.concatenate([ref[j : j + 1] for j in range(n)], axis=1)
    q = n // 4
    rows = []
    for j in range(q):
        t = ref[j : j + 1]
        for k in range(1, 4):
            t = jnp.where(y == k, ref[k * q + j : k * q + j + 1], t)
        rows.append(t)
    return jnp.concatenate(rows, axis=1)


def front(nav, doc_ref, gain_ref, post_ref, bias_row, loads, greeted, norm_piece, refs):
    (xv, cosv, sinv, wq, wk, wv, wo, part32, part16, got1, ss1, got_ss, s1, r1, s1b, r1b,
     kv, s3, r3, mixed, s5, r5, proj, got7, s7, r7, sq8, got8, s8, r8) = refs
    h, y, x = nav.h, nav.y, nav.x
    loads["x"].wait()
    xf = xv[...].astype(F32)
    scaled = (xf * row_of(gain_ref)).astype(BF)
    ss1[...] = lax.dot_general(
        jnp.ones((8, 1152), F32), xf * xf, (((1,), (1,)), ((), ())), precision=HIGHEST, preferred_element_type=F32
    )
    for name in ("q", "k", "v"):
        loads[name].wait()
    loads["dec"].start()
    loads["enc"].start()
    query = jnp.dot(scaled, wq[...], preferred_element_type=F32)
    key = jnp.dot(scaled, wk[...], preferred_element_type=F32)
    val = jnp.dot(scaled, wv[...], preferred_element_type=F32)
    for w in range(4):
        kvh = w // 2 * 128
        for k, t in enumerate((query[:, w * 128 : w * 128 + 128], key[:, kvh : kvh + 128], val[:, kvh : kvh + 128])):
            part32[w, :, k * 128 : k * 128 + 128] = t
            part16[w, :, k * 128 : k * 128 + 128] = t.astype(BF)
    greeted()
    square = [send(ss1, got_ss.at[d - 1], s1b.at[d - 1], r1b.at[d - 1], nav.peer("y", d)) for d in (1, 2, 3)]
    moved = {}
    for j, cols in enumerate((slice(128, 384), slice(0, 128))):
        for d in (2, 1, 3):
            moved[j, d] = send(
                part16.at[(y + d) % 4, :, cols], got1.at[d - 1, :, cols], s1.at[d - 1, j], r1.at[d - 1, j], nav.peer("y", d)
            )
    bounds = []
    run = 0
    for j in range(4):
        run = run + doc_ref[j]
        bounds.append(run)
    qpos = x * 128 + lax.broadcasted_iota(jnp.int32, (128, 512), 0)
    kpos = lax.broadcasted_iota(jnp.int32, (128, 512), 1)
    qseg = sum((b <= qpos).astype(jnp.int32) for b in bounds)
    kseg = sum((b <= kpos).astype(jnp.int32) for b in bounds)
    allowed = (qseg == kseg) & (kpos <= qpos)
    for copy in square:
        copy.wait_recv()
    total = ss1[...] + got_ss[0] + got_ss[1] + got_ss[2]
    spread = lax.dot_general(
        total, jnp.full((8, 128), 0.125, F32), (((0,), (0,)), ((), ())), precision=HIGHEST, preferred_element_type=F32
    )
    inverse = lax.rsqrt(spread / D + norm_eps)
    loads["cos"].wait()
    loads["sin"].wait()

    def whole_sum(k):
        cols = slice(k * 128, k * 128 + 128)
        t = part32[y, :, cols] + got1[0, :, cols].astype(F32) + got1[1, :, cols].astype(F32) + got1[2, :, cols].astype(F32)
        t = t * inverse
        if k < 2:
            t = t * cosv[...] + pltpu.roll(t, 64, 1) * sinv[...]
        return t.astype(BF)

    for d in (1, 2, 3):
        moved[0, d].wait_recv()
    kv[x, :, 0:128] = whole_sum(1)
    kv[x, :, 128:256] = whole_sum(2)
    later = []
    for d in (2, 1, 3):
        copy = pltpu.make_async_remote_copy(
            src_ref=kv.at[x], dst_ref=kv.at[x], send_sem=s3.at[d - 1], recv_sem=r3.at[d - 1],
            device_id=nav.peer("x", d), device_id_type=MESH,
        )
        pl.when(x + d < 4)(copy.start)
        later.append((d, copy))
    for d in (1, 2, 3):
        moved[1, d].wait_recv()
    own_query = whole_sum(0)
    loads["dec"].wait()
    norm_piece(0)
    for d, copy in later:
        pl.when(x >= d)(copy.wait_recv)
    keys = kv[:, :, 0:128].reshape(512, 128)
    vals = kv[:, :, 128:256].reshape(512, 128)
    scores = lax.dot_general(own_query, keys, (((1,), (1,)), ((), ())), preferred_element_type=F32) * ((D // HEADS) ** -0.5)
    capped = soft_cap * jnp.tanh(scores / soft_cap)
    weights = jnp.where(allowed, jnp.exp(capped), 0.0)
    probs = (weights / jnp.sum(weights, axis=-1, keepdims=True)).astype(BF)
    mixed[y] = jnp.dot(probs, vals, preferred_element_type=F32).astype(BF)
    mixes = [send(mixed.at[y], mixed.at[y], s5.at[d - 1], r5.at[d - 1], nav.peer("y", d)) for d in (2, 1, 3)]
    loads["o"].wait()
    for copy in mixes:
        copy.wait_recv()
    whole = jnp.concatenate([mixed[w] for w in range(4)], axis=1)
    for k in range(3):
        cols = slice(k * 384, k * 384 + 384)
        t = jnp.dot(whole, wo[:, cols], preferred_element_type=F32).astype(BF)
        proj[:, :, cols] = t.reshape(8, 16, 384)
    parts = [send(proj.at[(h + d) % 8], got7.at[d - 1], s7.at[d - 1], r7.at[d - 1], nav.peer("h", d)) for d in range(1, 8)]
    norm_piece(1)
    for copy in parts:
        copy.wait_recv()
    acc = proj[h].astype(F32)
    for d in range(7):
        acc = acc + got7[d].astype(F32)
    acc = acc.astype(BF).astype(F32)
    sq8[...] = jnp.broadcast_to(jnp.sum(acc * acc, axis=1, keepdims=True), (16, 128))
    norms = [send(sq8, got8.at[d - 1], s8.at[d - 1], r8.at[d - 1], nav.peer("y", d)) for d in (2, 1, 3)]
    norm_piece(2)
    for copy in norms:
        copy.wait_recv()
    inverse_post = lax.rsqrt((sq8[...] + got8[0] + got8[1] + got8[2]) / D + norm_eps)[:, 0:1]
    own_x = xv[pl.ds(pl.multiple_of(h * 16, 16), 16), :].astype(F32)
    resid = (own_x + acc * inverse_post * row_of(post_ref, y)).astype(BF)
    centered = (resid.astype(F32) - bias_row).astype(BF)
    sends = square + list(moved.values()) + mixes + parts + norms
    return resid, centered, sends, later


def step_kernel(
    doc_ref, gain_ref, post_ref, bias_ref, ebias_ref, x_hbm, cos_hbm, sin_hbm, wq_hbm, wk_hbm, wv_hbm, wo_hbm,
    enc_hbm, dec_hbm,
    cent_hbm, grad_hbm, flipped_ref, gpre_ref, coef_ref, loss_ref,
    acts_ref, enc, dec, lsem, osem, strips, ss, rs, errors, full, pre, norms, norm_row,
    part, got0, s0, r0, relay, got3, s3, r3, slab, got2, s2, r2, got1, s1, r1,
    pool_h, pool_y, pool_x, sl, rl, gfull, *rest,
):
    fsems, gsems, frefs = rest[:8], rest[8:16], rest[16:]
    nav = Nav()
    c, h, y, x = nav.c, nav.h, nav.y, nav.x
    place = [[nav.index(a) for a in order] for order in ORDERS]
    rows = pl.ds(pl.multiple_of(x * 128, 128), 128)
    xv, cosv, sinv, wq, wk, wv, wo = frefs[:7]
    loads = {}
    for k, (name, src, dst) in enumerate([
        ("x", x_hbm.at[rows], xv), ("q", wq_hbm, wq), ("k", wk_hbm, wk), ("v", wv_hbm, wv),
        ("cos", cos_hbm.at[rows], cosv), ("sin", sin_hbm.at[rows], sinv), ("o", wo_hbm, wo),
        ("dec", dec_hbm, dec), ("enc", enc_hbm, enc),
    ]):
        loads[name] = pltpu.make_async_copy(src, dst, lsem.at[k])
        if k < 7:
            loads[name].start()
    kv = frefs[16]
    kv[...] = jnp.zeros(kv.shape, BF)
    greeted = greet(nav)

    def norm_piece(k):
        if k == 2:
            sums = lax.dot_general(
                jnp.ones((8, 128), F32), norms[...], (((1,), (1,)), ((), ())), precision=HIGHEST, preferred_element_type=F32
            )
            norm_row[...] = jnp.sqrt(sums + norm_eps)
            pre[...] = jnp.zeros(pre.shape, F32)
            return

        def body(j, carry):
            r = pl.ds(pl.multiple_of(j * 32, 32), 32)
            t = jnp.zeros((32, 128), F32)
            for m in range(36):
                v = dec[r, m * 128 : m * 128 + 128].astype(F32)
                t = t + v * v
            norms[r, :] = t
            return carry

        lax.fori_loop(k * 8, k * 8 + 8, body, 0)

    bias_row = row_of(bias_ref, y)
    resid, centered, sends, later = front(nav, doc_ref, gain_ref, post_ref, bias_row, loads, greeted, norm_piece, frefs[:-1])
    for p in range(3):
        i1, i2, i3 = place[p]
        full[p, c, i3, i2, i1] = centered[:, p * 384 : p * 384 + 384]
        strips[p, i1] = resid[:, p * 384 : p * 384 + 384]

    def before_encode(k):
        if k == 2:
            loads["enc"].wait()

    def encode(p, ks):
        def product(ws, left):
            rows = jnp.concatenate([enc[columns(w, p), :] for w in ws], axis=0)
            return jnp.dot(left, rows, preferred_element_type=F32)

        slab_product(p, ks, full, product, pre)
        for k in ks:
            unpack(full, cent_hbm, osem.at[0], p, k)

    drain_full = all_gather(nav, full, fsems, before_encode, encode)
    known = {}
    for p, order in enumerate(ORDERS):
        mine = strips.at[p, place[p][0]]
        for d in (2, 1, 3):
            known[p, d] = send(mine, mine, ss.at[p, d - 1], rs.at[p, d - 1], nav.peer(order[0], d))
    act_sum = jnp.zeros((1, 512), F32)
    ebias = row_of(ebias_ref)
    for k in range(2):
        t = flat(pre[k]) + ebias
        pre[k] = t.reshape(4, 4, 16, 512)
        acts = jnp.maximum(t, 0.0).astype(BF)
        acts_ref[k] = acts.reshape(4, 4, 16, 512)
        act_sum = act_sum + jnp.sum(acts.astype(F32), axis=0, keepdims=True)
    penalty = jnp.sum(act_sum * norm_row[0:1], keepdims=True)
    coef_ref[...] = (l1_weight / TOKENS) * act_sum / norm_row[...]

    swap, third, second, first = {}, {}, {}, {}

    def exchange(p, d):
        t3 = (place[p][2] + d) % 4
        swap[p, d] = send(part.at[p, 1 - c, t3], got0.at[p, t3], s0.at[p, d], r0.at[p, d], nav.peer("c", 1))

    def produce(p, *ws):
        cols = jnp.concatenate([dec[:, columns(w, p)] for w in ws], axis=1)
        both = jnp.dot(flat(acts_ref[...]), cols, preferred_element_type=F32).astype(BF)
        for j, w in enumerate(ws):
            t = both[:, j * 384 : j * 384 + 384].reshape(2, 4, 4, 16, 384)
            part[1, :, w] = t

    def out3(p, slot, src, dst, d):
        third[p, slot] = send(src, dst, s3.at[p, slot], r3.at[p, slot], nav.peer(ORDERS[p][2], d))

    def chip_sum(p, t3, k):
        return part[p, c, t3, k : k + 2].astype(F32) + got0[p, t3, k : k + 2].astype(F32)

    def far(p):
        t3 = (place[p][2] + 2) % 4
        swap[p, 2].wait_recv()
        for k, d in ((0, 1), (2, 3)):
            half = part.at[p, c, t3, k : k + 2]
            half[...] = chip_sum(p, t3, k).astype(BF)
            out3(p, k // 2, half, relay.at[p, k // 2], d)

    def near(p):
        for d, k in ((1, 2), (3, 0)):
            t3 = (place[p][2] + d) % 4
            swap[p, d].wait_recv()
            half = part.at[p, c, t3, k : k + 2]
            half[...] = chip_sum(p, t3, k).astype(BF)
            out3(p, d + 1, half, got3.at[p, d // 2, k : k + 2], d)

    def joined(p):
        for d, k in ((1, 0), (3, 2)):
            t3 = (place[p][2] + d) % 4
            third[p, d // 2].wait_recv()
            half = part.at[p, c, t3, k : k + 2]
            half[...] = (chip_sum(p, t3, k) + relay[p, d // 2].astype(F32)).astype(BF)
            out3(p, d + 2, half, got3.at[p, d // 2, k : k + 2], d)

    def produce_rows(p, ds, ws):
        ts = [(place[p][2] + d) % 4 for d in ds]
        left = jnp.concatenate([flat(acts_ref[slab_rows(p, t) + (Ellipsis,)]) for t in ts], axis=0)
        cols = jnp.concatenate([dec[:, columns(w, p)] for w in ws], axis=1)
        both = jnp.dot(left, cols, preferred_element_type=F32).astype(BF)
        for j, t3 in enumerate(ts):
            for i, w in enumerate(ws):
                t = both[j * 128 : j * 128 + 128, i * 384 : i * 384 + 384].reshape(2, 4, 16, 384)
                if p == 0:
                    part[0, :, t3, :, w] = t
                else:
                    part[2, :, t3, w] = t

    produce(1, (y + 2) % 4)
    exchange(1, 2)
    produce_rows(0, (2,), range(4))
    exchange(0, 2)
    produce_rows(2, (2,), range(4))
    exchange(2, 2)
    far(1)
    produce(1, (y + 1) % 4, (y + 3) % 4)
    exchange(1, 1)
    exchange(1, 3)
    far(0)
    far(2)
    produce_rows(0, (1, 3, 0), (0, 1))
    near(1)
    produce_rows(0, (1, 3, 0), (2, 3))
    for d in (1, 3, 0):
        exchange(0, d)
    produce_rows(2, (1, 3, 0), (0, 1))
    near(0)
    produce_rows(2, (1, 3, 0), (2, 3))
    for d in (1, 3, 0):
        exchange(2, d)
    joined(1)
    produce(1, y)
    exchange(1, 0)
    near(2)
    joined(0)
    for k in range(2):
        flipped_ref[:, k * 256 : k * 256 + 256] = flat(acts_ref[k]).T
    joined(2)
    for p in range(3):
        swap[p, 0].wait_recv()
    for p in range(3):
        i1, i2, i3 = place[p]
        for slot in (2, 3, 4, 5):
            third[p, slot].wait_recv()
        t = part[p, c, i3].astype(F32) + got0[p, i3].astype(F32)
        t = t + got3[p, 0].astype(F32) + got3[p, 1].astype(F32)
        slab[p] = t.astype(BF)
        for d in (2, 1, 3):
            second[p, d] = send(slab.at[p, (i2 + d) % 4], got2.at[p, d - 1], s2.at[p, d - 1], r2.at[p, d - 1], nav.peer(ORDERS[p][1], d))
    for p in range(3):
        i1, i2, i3 = place[p]
        for d in (1, 2, 3):
            second[p, d].wait_recv()
        t = slab[p, i2].astype(F32)
        for d in range(3):
            t = t + got2[p, d].astype(F32)
        mine = got1.at[p, i1]
        mine[...] = t.astype(BF)
        for d in (2, 1, 3):
            first[p, d] = send(mine, mine, s1.at[p, d - 1], r1.at[p, d - 1], nav.peer(ORDERS[p][0], d))
    squares = jnp.zeros((16, 384), F32)
    for p in range(3):
        i1, i2, i3 = place[p]
        for d in (1, 2, 3):
            first[p, d].wait_recv()
            known[p, d].wait_recv()
        for j in range(4):
            t = got1[p, 0, j].astype(F32)
            for k in range(1, 4):
                t = t + got1[p, k, j].astype(F32)
            if p == 0:
                bias = jnp.concatenate([bias_ref[j * 9 + k : j * 9 + k + 1] for k in range(3)], axis=1)
            else:
                bias = bias_row[:, p * 384 : p * 384 + 384]
            error = t + bias - strips[p, j].astype(F32)
            errors[j] = error
            gfull[p, c, i3, i2, j] = (2.0 / TOKENS * error).astype(BF)
        own = errors[i1]
        squares = squares + own * own

    pools = [(pool_h, "h", 8, h), (pool_y, "y", 4, y), (pool_x, "x", 4, x)]
    losses = []

    def pool_send(k):
        pool, axis, n, me = pools[k]
        for d in range(1, n):
            losses.append(send(pool.at[me], pool.at[me], sl.at[k, d - 1], rl.at[k, d - 1], nav.peer(axis, d)))

    def pool_sum(k):
        pool, axis, n, me = pools[k]
        for copy in losses[-(n - 1) :]:
            copy.wait_recv()
        total = pool[0]
        for j in range(1, n):
            total = total + pool[j]
        return total

    def loss_filler(k):
        if k == 0:
            pool_h[h] = jnp.broadcast_to(jnp.sum(squares, keepdims=True), (8, 128)) + l1_weight * penalty
            pool_send(0)
        if k == 1:
            pool_y[y] = pool_sum(0)
            pool_send(1)
        if k == 2:
            pool_x[x] = pool_sum(1)
            pool_send(2)

    upstream = frefs[-1]
    upstream[...] = jnp.zeros(upstream.shape, F32)

    def decode(p, ks):
        def product(ws, left):
            cols = jnp.concatenate([dec[:, columns(w, p)] for w in ws], axis=1)
            return lax.dot_general(left, cols, (((1,), (1,)), ((), ())), preferred_element_type=F32)

        slab_product(p, ks, gfull, product, upstream)
        for k in ks:
            unpack(gfull, grad_hbm, osem.at[1], p, k)

    drain_gfull = all_gather(nav, gfull, gsems, loss_filler, decode, whole_strips=True)
    loss_ref[...] = pool_sum(2) / (TOKENS * D)
    lift = (l1_weight / TOKENS) * norm_row[0:1]
    for k in range(2):
        t = jnp.where(flat(pre[k]) > 0, flat(upstream[k]) + lift, 0.0).astype(BF)
        gpre_ref[k] = t.reshape(4, 4, 16, 512)
    drain_full()
    drain_gfull()
    for group in (swap, third, second, first, known):
        for copy in group.values():
            copy.wait_send()
    for copy in losses + sends:
        copy.wait_send()
    for d, copy in later:
        pl.when(x + d < 4)(copy.wait_send)
    pltpu.make_async_copy(cent_hbm, cent_hbm, osem.at[0]).wait()
    pltpu.make_async_copy(grad_hbm, grad_hbm, osem.at[1]).wait()


def step(*args):
    dma = pltpu.SemaphoreType.DMA
    vmem = pl.BlockSpec(memory_space=pltpu.VMEM)
    anyspace = pl.BlockSpec(memory_space=pl.ANY)
    V = pltpu.VMEM
    front_scratch = [
        V((128, 1152), BF), V((128, 128), F32), V((128, 128), F32),
        V((1152, 512), BF), V((1152, 256), BF), V((1152, 256), BF), V((512, 1152), BF),
        V((4, 128, 384), F32), V((4, 128, 384), BF), V((3, 128, 384), BF),
        V((8, 128), F32), V((3, 8, 128), F32), dma((3, 2)), dma((3, 2)), dma((3,)), dma((3,)),
        V((4, 128, 256), BF), dma((3,)), dma((3,)),
        V((4, 128, 128), BF), dma((3,)), dma((3,)),
        V((8, 16, 1152), BF), V((7, 16, 1152), BF), dma((7,)), dma((7,)),
        V((16, 128), F32), V((3, 16, 128), F32), dma((3,)), dma((3,)),
    ]
    return pl.pallas_call(
        step_kernel,
        name="step",
        out_shape=(
            jax.ShapeDtypeStruct((2, 4, 4, 16, D), BF), jax.ShapeDtypeStruct((2, 4, 4, 16, D), BF),
            jax.ShapeDtypeStruct((512, 512), BF), jax.ShapeDtypeStruct((2, 4, 4, 16, 512), BF),
            jax.ShapeDtypeStruct((8, 512), F32), jax.ShapeDtypeStruct((8, 128), F32),
        ),
        in_specs=[pl.BlockSpec(memory_space=pltpu.SMEM)] + [vmem] * 4 + [anyspace] * 9,
        out_specs=(anyspace, anyspace, vmem, vmem, vmem, vmem),
        scratch_shapes=[
            V((2, 4, 4, 16, 512), BF), V((D, 512), BF), V((512, D), BF), dma((9,)), dma((2,)), V((3, 4, 16, 384), BF), dma((3, 3)), dma((3, 3)), V((4, 16, 384), F32),
            V((3, 2, 4, 4, 4, 16, 384), BF), V((2, 4, 4, 16, 512), F32), V((512, 128), F32), V((8, 512), F32),
            V((3, 2, 4, 4, 4, 16, 384), BF), V((3, 4, 4, 4, 16, 384), BF), dma((3, 4)), dma((3, 4)),
            V((3, 2, 2, 4, 16, 384), BF), V((3, 2, 4, 4, 16, 384), BF), dma((3, 6)), dma((3, 6)),
            V((3, 4, 4, 16, 384), BF), V((3, 3, 4, 16, 384), BF), dma((3, 3)), dma((3, 3)),
            V((3, 4, 4, 16, 384), BF), dma((3, 3)), dma((3, 3)),
            V((8, 8, 128), F32), V((4, 8, 128), F32), V((4, 8, 128), F32), dma((3, 7)), dma((3, 7)),
            V((3, 2, 4, 4, 4, 16, 384), BF),
        ] + gather_sems() + gather_sems() + front_scratch + [V((2, 4, 4, 16, 512), F32)],
        compiler_params=pltpu.CompilerParams(collective_id=0, has_side_effects=True, vmem_limit_bytes=60 << 20),
    )(*args)


def grads_kernel(cent_ref, gpre_ref, grad_ref, flipped_ref, dec_ref, coef_ref, loss_in, genc_ref, gdec_ref, loss_out, lift):
    @pl.when(pl.program_id(0) == 0)
    def _():
        lift[...] = lax.dot_general(
            coef_ref[...], jnp.full((8, 128), 0.125, F32), (((0,), (0,)), ((), ())), precision=HIGHEST, preferred_element_type=F32
        )
        loss_out[0, 0] = loss_in[0, 0]

    t = jnp.dot(flipped_ref[...], grad_ref[...], preferred_element_type=F32)
    for m in range(t.shape[1] // 128):
        cols = slice(m * 128, m * 128 + 128)
        gdec_ref[:, cols] = (t[:, cols] + lift[...] * dec_ref[:, cols].astype(F32)).astype(BF)
    genc_ref[...] = lax.dot_general(
        cent_ref[...], gpre_ref[...], (((0,), (0,)), ((), ())), preferred_element_type=F32
    ).astype(BF)


def grads(centered, grad_pre, grad_recon, acts, dec, coef, loss):
    tall = pl.BlockSpec((512, 768), lambda j: (0, j))
    square = pl.BlockSpec((512, 512), lambda j: (0, 0))
    return pl.pallas_call(
        grads_kernel,
        name="grads",
        grid=(6,),
        out_shape=(
            jax.ShapeDtypeStruct((D, 512), BF), jax.ShapeDtypeStruct((512, D), BF), jax.ShapeDtypeStruct((1, 1), F32)
        ),
        in_specs=[
            tall, square, tall, square, tall, pl.BlockSpec((8, 512), lambda j: (0, 0)), pl.BlockSpec(memory_space=pltpu.SMEM),
        ],
        out_specs=(pl.BlockSpec((768, 512), lambda j: (j, 0)), tall, pl.BlockSpec(memory_space=pltpu.SMEM)),
        scratch_shapes=[pltpu.VMEM((512, 128), F32)],
        compiler_params=pltpu.CompilerParams(dimension_semantics=("arbitrary",), vmem_limit_bytes=63 << 20),
    )(centered, grad_pre, grad_recon, acts, dec, coef, loss)


def rope_tables():
    j = np.arange(HEAD_DIM // 2, dtype=np.float32)
    frequency = np.power(np.float32(rope_base), np.float32(-2.0) * j / np.float32(HEAD_DIM)).astype(np.float32)
    angles = (np.arange(TOKENS, dtype=np.float32)[:, None] * frequency[None, :]).astype(np.float32)
    cos, sin = np.cos(angles).astype(np.float32), np.sin(angles).astype(np.float32)
    return np.concatenate([cos, cos], 1), np.concatenate([-sin, sin], 1)


def per_device(
    x_in, doc_lengths, attn_gain, w_query, w_key, w_value, w_out, post_gain, enc_weight, enc_bias, dec_weight, dec_bias
):
    cos, sin = rope_tables()
    centered, grad_recon, acts, grad_pre, coef, loss = step(
        doc_lengths, attn_gain.reshape(9, 128), post_gain.reshape(36, 128), dec_bias.reshape(36, 128),
        enc_bias.reshape(4, 128), x_in, jnp.asarray(cos), jnp.asarray(sin),
        w_query, w_key, w_value, w_out, enc_weight, dec_weight,
    )
    centered, grad_recon = centered.reshape(TOKENS, D), grad_recon.reshape(TOKENS, D)
    grad_pre = grad_pre.reshape(TOKENS, 512)
    grad_enc, grad_dec, total = grads(centered, grad_pre, grad_recon, acts, dec_weight, coef, loss)
    return (grad_enc, grad_dec, total.reshape(()))


def solution(mesh):
    placed = (
        P(None, "width"),
        P(),
        P("width"),
        P("width", "heads"),
        P("width", "heads"),
        P("width", "heads"),
        P("heads", "width"),
        P(),
        P(None, ("heads", "width", "sae")),
        P(("heads", "width", "sae")),
        P(("heads", "width", "sae"), None),
        P(),
    )
    return jax.shard_map(
        per_device,
        mesh=mesh,
        in_specs=placed,
        out_specs=(P(None, ("heads", "width", "sae")), P(("heads", "width", "sae"), None), P()),
        check_vma=False,
    )
```
